256 devices in a mesh: dp: 8 (over z), label: 32 (over y, x, core).
Axes of the slice: x: 4, y: 4, z: 8, core: 2. Of those that a mesh axis runs over, the one named last changes fastest.
Arguments:
- enc: bfloat16 [262144, 768], P(('dp', 'label')), may hold values from -6 to 6
- proj: bfloat16 [768, 768], replicated, may hold values from -0.21875 to 0.21875
- head_weight: bfloat16 [4096, 768], P('label'), may hold values from -0.21875 to 0.21875
- shortlist: int32 [2048, 4], P(('dp', 'label')), may hold values from 0 to 31, all different within a row; in each aligned block of 8 rows (0 to 7, 8 to 15, ...) at most 2 rows name the same one
- positives: int32 [262144, 8], P(('dp', 'label')), may hold values from 0 to 511
- weight_num: int32 [4096], P('label'), may hold values from 1 to 16
- weight_den: int32 [4096], P('label'), may hold values from 1 to 16
Outputs:
- grad_enc: float32 [262144, 768], P(('dp', 'label'))
- grad_proj: float32 [768, 768], replicated
- grad_head: float32 [4096, 768], P('label', 'dp')
The draws below stay inside these ranges and needn't reach their ends.
Inputs may be any that keep to these rules, and one draw needn't show every extreme that they name: `shortlist`: each row names 4 different clusters; among the rows of one device no cluster is named by more than 2 rows, and in every draw some cluster is named by exactly 2 rows of some device; every cluster is named somewhere.
All inputs are finite; a program needn't handle non-finite values.
Results may differ from the reference program's by a relative error of at most 0.005.
Values may be sent and summed in bfloat16 or wider, within the bound.
A program may use at most 128 MiB of HBM per device.

```python
import math
import jax
import jax.numpy as jnp
import numpy as np
from jax import lax

D = 768
LB = 128
SB = 128
BEAM = 4
POS = 8
BLK_DEV = 8
CAP = 2
CLUSTERS = 32
LABELS = 4096
BLOCKS = 2048
SAMPLES = 262144


def touch_ends(values, key, low, high):
    spot = [jax.random.randint(jax.random.fold_in(key, axis), (), 0, length) for axis, length in enumerate(values.shape)]
    main_axis = values.shape.index(max(values.shape))
    neighbour = spot[:main_axis] + [(spot[main_axis] + 1) % values.shape[main_axis]] + spot[main_axis + 1:]
    return values.at[tuple(spot)].set(low).at[tuple(neighbour)].set(high)


def steps_of(stream_key, shape, shards, low, top_value):
    level, own = 1.0, jax.random.fold_in(stream_key, 6)
    for axis_at, blocks in shards:
        heights = jnp.exp(jax.random.uniform(jax.random.fold_in(own, axis_at), (blocks,), jnp.float32, low / len(shards), top_value / len(shards)))
        level = level * jnp.repeat(heights, shape[axis_at] // blocks).reshape([-1 if axis == axis_at else 1 for axis in range(len(shape))])
    return level


def shared_out(stream_key, own, number, rows, count, top, bound, lean):
    ranking = jax.random.permutation(stream_key, count)
    heavy_load, usual = shares(count, rows * top, bound, lean, True), shares(count, rows * top, bound, lean, False)
    places = jnp.arange(count)

    def named(tallies, rotation):
        used = int((tallies > 0).sum())
        fixed = max(1, used // 4)
        moved = fixed + (places - fixed + rotation * (used - fixed)) % max(1, count - fixed)
        return jnp.zeros((count,), jnp.int32).at[ranking[jnp.where(places < fixed, places, moved)]].set(jnp.asarray(tallies, jnp.int32))

    tallies = jnp.where(number % 4 == 0, named(heavy_load, number // 4), named(usual, number - number // 4 - 1))
    mixed = jax.random.permutation(jax.random.fold_in(own, 3), count)
    giver, taker = mixed[0:count // 2 * 2:2], mixed[1:count // 2 * 2:2]
    slack = jnp.minimum(tallies[giver] - 1, bound - tallies[taker]) // 2
    slack = jnp.where((giver == ranking[0]) | (taker == ranking[0]) | (tallies[taker] == 0), 0, jnp.maximum(slack, 0))
    moved = jax.random.randint(jax.random.fold_in(own, 4), (count // 2,), 0, 1 << 20) % (slack + 1)
    tallies = tallies.at[giver].add(-moved).at[taker].add(moved)
    items = jnp.searchsorted(jnp.cumsum(tallies), jnp.arange(rows * top), side="right").astype(jnp.int32)
    table = items.reshape(top, rows).T
    table = table[jax.random.permutation(jax.random.fold_in(own, 1), rows)]
    rotation = jax.random.randint(jax.random.fold_in(own, 2), (rows, 1), 0, top)
    return jnp.take_along_axis(table, (jnp.arange(top)[None, :] + rotation) % top, axis=1)


def shares(number_of, total, most, skew, full):
    weights = [(1 << 20) // math.isqrt(rank ** skew) + 1 for rank in range(1, number_of + 1)]
    largest = most if full else min(most, max(-(-total // number_of), total * weights[0] // sum(weights)))
    least = 1 if total - largest >= number_of - 1 else 0
    given, surplus = [largest] + [least] * (number_of - 1), total - largest - least * (number_of - 1)
    while surplus > 0:
        movable = [i for i in range(1, number_of) if given[i] < largest] or [i for i in range(1, number_of) if given[i] < most]
        pool, budget = sum([weights[i] for i in movable]), surplus
        for i in movable:
            more = min(most - given[i], max(1, budget * weights[i] // pool), surplus)
            given[i] = given[i] + more
            surplus = surplus - more
    return np.array(given)


def scatter_about(rng, shape, deviation, most, cuts=(), kind=jnp.bfloat16):
    values = jax.random.normal(rng, shape, jnp.float32) * deviation
    if len(cuts) > 0:
        values = steps_of(rng, shape, cuts, -0.22, 0.18) * values
    return jnp.clip(values, min=-most, max=most).astype(kind)


def setup_inputs(seed: int = 0) -> dict:
    key_of = jax.random.split(jax.random.key(seed), 8)
    enc = scatter_about(key_of[0], (SAMPLES, D), 1.0, 6.0, ((0, 256),))
    proj = scatter_about(key_of[1], (D, D), D ** -0.5, 0.21875)
    head_weight = scatter_about(key_of[2], (LABELS, D), D ** -0.5, 0.21875, ((0, 32),))
    shortlist_keys = jax.random.split(jax.random.fold_in(key_of[3], 1), BLOCKS // BLK_DEV)
    shortlist_turns = jax.random.permutation(jax.random.fold_in(key_of[3], 3), BLOCKS // BLK_DEV)
    shortlist = jax.vmap(lambda own, number: shared_out(jax.random.fold_in(key_of[3], 2), own, number, BLK_DEV, CLUSTERS, BEAM, CAP, 2))(shortlist_keys, shortlist_turns).reshape((BLOCKS, BEAM))
    positives = touch_ends(jax.random.randint(key_of[4], (SAMPLES, POS), 0, BEAM * LB), jax.random.fold_in(key_of[4], 1), 0, (BEAM * LB) - 1).astype(jnp.int32)
    weight_num = touch_ends(jax.random.randint(key_of[5], (LABELS,), 1, 17), jax.random.fold_in(key_of[5], 1), 1, 16).astype(jnp.int32)
    weight_den = touch_ends(jax.random.randint(key_of[6], (LABELS,), 1, 17), jax.random.fold_in(key_of[6], 1), 1, 16).astype(jnp.int32)
    return dict(enc=enc, proj=proj, head_weight=head_weight, shortlist=shortlist, positives=positives, weight_num=weight_num, weight_den=weight_den)


def contract(left, right, left_dim, right_dim):
    return lax.dot_general(left, right, (((left_dim,), (right_dim,)), ((), ())), preferred_element_type=jnp.float32)


def reference(enc, proj, head_weight, shortlist, positives, weight_num, weight_den):
    label_weight = weight_num.astype(jnp.float32) / weight_den.astype(jnp.float32)
    label_iota = jnp.arange(LB, dtype=jnp.int32)
    enc_blocks = enc.reshape(BLOCKS, SB, D)
    pos_blocks = positives.reshape(BLOCKS, SB, POS)

    def one_block(carried, inputs):
        grad_head, grad_proj = carried
        block_rows, picked, wanted = inputs
        hidden = jnp.dot(block_rows, proj, preferred_element_type=jnp.float32).astype(jnp.bfloat16)
        grad_hidden = jnp.zeros((SB, D), jnp.float32)
        for beam_slot in range(BEAM):
            row_start = (picked[beam_slot] * LB).astype(jnp.int32)
            cluster_rows = lax.dynamic_slice_in_dim(head_weight, row_start, LB, 0)
            cluster_scale = lax.dynamic_slice_in_dim(label_weight, row_start, LB, 0)
            logits = contract(hidden, cluster_rows, 1, 1)
            shifted = wanted - beam_slot * LB
            target = jnp.zeros((SB, LB), jnp.bool_)
            for column in range(POS):
                target = target | (shifted[:, column, None] == label_iota[None, :])
            grad_logits = (cluster_scale[None, :] * (jax.nn.sigmoid(logits) - target.astype(jnp.float32)) / SB).astype(jnp.bfloat16)
            grad_part = jnp.dot(grad_logits, cluster_rows, preferred_element_type=jnp.float32).astype(jnp.bfloat16)
            grad_part = lax.optimization_barrier(grad_part)
            grad_hidden = grad_hidden + grad_part.astype(jnp.float32)
            update = contract(grad_logits, hidden, 0, 0)
            current = lax.dynamic_slice_in_dim(grad_head, row_start, LB, 0)
            grad_head = lax.dynamic_update_slice_in_dim(grad_head, current + update, row_start, 0)
        grad_hidden = grad_hidden.astype(jnp.bfloat16)
        grad_rows = contract(grad_hidden, proj, 1, 1)
        grad_proj = grad_proj + contract(block_rows, grad_hidden, 0, 0)
        return (grad_head, grad_proj), grad_rows

    start_carry = (jnp.zeros((LABELS, D), jnp.float32), jnp.zeros((D, D), jnp.float32))
    (grad_head, grad_proj), grad_rows = lax.scan(one_block, start_carry, (enc_blocks, shortlist, pos_blocks))
    return grad_rows.reshape(SAMPLES, D), grad_proj, grad_head
```

```python
import jax
import jax.numpy as jnp
from jax import lax
from jax.sharding import PartitionSpec as P


def shards(enc, proj, head_weight, shortlist, positives, weight_num, weight_den):
    block_count, beam_width = shortlist.shape
    samples, width = enc.shape
    rows = samples // block_count
    size = head_weight.shape[0]
    clusters = lax.axis_size("label")
    weights = lax.all_gather(head_weight, "label")
    scale = weight_num.astype(jnp.float32) / weight_den.astype(jnp.float32)
    scales = lax.all_gather(scale, "label")
    hidden = jnp.dot(enc, proj, preferred_element_type=jnp.float32).astype(jnp.bfloat16)
    blocks = hidden.reshape(block_count, rows, width)
    picked = jnp.take(weights, shortlist.reshape(-1), axis=0).reshape(
        block_count, beam_width * size, width
    )
    picked_scale = jnp.take(scales, shortlist.reshape(-1), axis=0).reshape(
        block_count, 1, beam_width * size
    )
    logits = jnp.einsum("bsd,bld->bsl", blocks, picked, preferred_element_type=jnp.float32)
    place = jnp.arange(beam_width * size, dtype=jnp.int32)
    wanted = positives.reshape(block_count, rows, -1)
    target = jnp.zeros(logits.shape, jnp.bool_)
    for column in range(wanted.shape[2]):
        target = target | (wanted[:, :, column, None] == place)
    grad_logits = (
        picked_scale * (jax.nn.sigmoid(logits) - target.astype(jnp.float32)) / rows
    ).astype(jnp.bfloat16)
    grad_hidden = jnp.einsum(
        "bsl,bld->bsd", grad_logits, picked, preferred_element_type=jnp.float32
    ).astype(jnp.bfloat16).reshape(samples, width)
    grad_pair = jnp.einsum(
        "bsl,bsd->bld", grad_logits, blocks, preferred_element_type=jnp.float32
    ).astype(jnp.bfloat16).reshape(block_count * beam_width, size, width)
    chosen = (shortlist.reshape(1, -1) == jnp.arange(clusters, dtype=jnp.int32)[:, None]).astype(
        jnp.bfloat16
    )
    grad_all = jnp.einsum("cp,pld->cld", chosen, grad_pair, preferred_element_type=jnp.float32)
    grad_enc = lax.dot_general(
        grad_hidden, proj, (((1,), (1,)), ((), ())), preferred_element_type=jnp.float32
    )
    grad_proj = lax.psum(
        lax.dot_general(
            enc, grad_hidden, (((0,), (0,)), ((), ())), preferred_element_type=jnp.float32
        ),
        ("dp", "label"),
    )
    grad_rows = lax.psum_scatter(grad_all, "label", scatter_dimension=0, tiled=False)
    grad_head = lax.psum_scatter(grad_rows, "dp", scatter_dimension=1, tiled=True)
    return (grad_enc, grad_proj, grad_head)


def solution(mesh):
    placed = (
        P(("dp", "label"), None),
        P(),
        P("label", None),
        P(("dp", "label"), None),
        P(("dp", "label"), None),
        P("label"),
        P("label"),
    )
    return jax.shard_map(
        shards,
        mesh=mesh,
        in_specs=placed,
        out_specs=(P(("dp", "label"), None), P(), P("label", "dp")),
        check_vma=False,
    )
```

```python
import jax
import jax.numpy as jnp
from jax import lax
from jax.experimental import pallas as pl
from jax.experimental.pallas import tpu as pltpu
from jax.sharding import PartitionSpec as P

MESH = pl.DeviceIdType.MESH
F32 = jnp.float32
BF16 = jnp.bfloat16

D = 768
LB = 128
SB = 128
BEAM = 4
NBLK = 8
ROWS = NBLK * SB
SHARD = D + 16
HALF0, HALF1 = 400, 384
NZ = 8
PIECE = 144
ABLK = 4 * PIECE
CORE = 4 * ABLK


def lid(pa, pb, core):
    xx = pa + core * (pb - pa)
    yy = pb + core * (pa - pb)
    return (yy * 4 + xx) * 2 + core


def kernel(
    sl, tab, live, enc, proj, shard, pos,
    ge_out, gp_out, gh_out,
    wl, hid, hidt, enct, w4, gl, gh, ge,
    sb, rb, cb, cf, r1a, r1b, s2p, s2m, r2p, r2m,
    db0, t1a, t1b, u2p, u2m, v2p, v2m, ef, zs, zr,
    ps0, pr0, pf, pa1, p1a, p1b, ps2p, ps2m, pr2p, pr2m,
    pb0, q1a, q1b, qs2p, qs2m, qr2p, qr2m, ez, zp, po,
    ss, rs, ls,
):
    z = lax.axis_index("dp")
    me = lax.axis_index("label")
    core = me % 2
    x = (me // 2) % 4
    y = me // 8
    pa = x + core * (y - x)
    pb = y + core * (x - y)
    other = 1 - core
    ap, am = (pa + 1) % 4, (pa + 3) % 4
    bp, bm = (pb + 1) % 4, (pb + 3) % 4
    a2, b2 = (pa + 2) % 4, (pb + 2) % 4
    sib = {"label": me + 1 - 2 * core}
    to_ap = {"label": lid(ap, pb, core)}
    to_am = {"label": lid(am, pb, core)}
    to_bp = {"label": lid(pa, bp, core)}
    to_bm = {"label": lid(pa, bm, core)}
    to_z = [None] + [{"dp": (z + dz) % NZ} for dz in range(1, NZ)]

    barrier = pltpu.get_barrier_semaphore()
    greeted = [sib, to_ap, to_am, to_bp, to_bm] + to_z[1:]
    for device in greeted:
        pl.semaphore_signal(barrier, inc=1, device_id=device, device_id_type=MESH)
    pl.semaphore_wait(barrier, len(greeted))

    count = [0]
    sent = []

    def take(n=1):
        first = count[0]
        count[0] += n
        return first

    def remote(src, dst, i, device):
        return pltpu.make_async_remote_copy(
            src_ref=src, dst_ref=dst, send_sem=ss.at[i], recv_sem=rs.at[i],
            device_id=device, device_id_type=MESH,
        )

    def send(src, dst, i, device):
        copy = remote(src, dst, i, device)
        copy.start()
        sent.append(copy)

    def landed(dst, i):
        remote(dst, dst, i, sib).wait_recv()

    def hidden_chunk(i):
        rows = enc[pl.ds(256 * i, 256), :]
        value = jnp.dot(rows, proj[...], preferred_element_type=F32).astype(BF16)
        hid[2 * i] = value[:SB]
        hid[2 * i + 1] = value[SB:]
        hidt[2 * i] = value[:SB].T
        hidt[2 * i + 1] = value[SB:].T
        enct[:, pl.ds(256 * i, 256)] = rows.T

    first = wl.at[pl.ds(0, 1)]
    del first
    own = pltpu.make_async_copy(shard, wl.at[me], ls.at[0])
    own.start()
    top, bottom = pl.ds(0, HALF0), pl.ds(HALF0, HALF1)
    base = take(20)
    near = take(16)

    def slot(a, b):
        return wl.at[lid(a, b, core)]

    columns = [pa, am, ap, a2]
    source = [shard, slot(am, pb), slot(ap, pb), slot(a2, pb)]
    send(shard, wl.at[me], base + 0, to_ap)
    send(shard, wl.at[me], base + 1, to_am)
    send(shard, wl.at[me], base + 4, to_bp)
    send(shard, wl.at[me], base + 5, to_bm)
    send(shard, wl.at[me], near + 0, sib)
    hidden_chunk(0)
    landed(slot(am, pb), base + 0)
    send(slot(am, pb).at[top], slot(am, pb).at[top], base + 2, to_ap)
    send(slot(am, pb), slot(am, pb), base + 8, to_bp)
    send(slot(am, pb), slot(am, pb), base + 9, to_bm)
    send(slot(am, pb), slot(am, pb), near + 1, sib)
    landed(slot(ap, pb), base + 1)
    send(slot(ap, pb).at[bottom], slot(ap, pb).at[bottom], base + 3, to_am)
    send(slot(ap, pb), slot(ap, pb), base + 12, to_bp)
    send(slot(ap, pb), slot(ap, pb), base + 13, to_bm)
    send(slot(ap, pb), slot(ap, pb), near + 2, sib)
    landed(slot(pa, bm), base + 4)
    send(slot(pa, bm).at[top], slot(pa, bm).at[top], base + 6, to_bp)
    send(slot(pa, bm), slot(pa, bm), near + 4, sib)
    landed(slot(pa, bp), base + 5)
    send(slot(pa, bp).at[bottom], slot(pa, bp).at[bottom], base + 7, to_bm)
    send(slot(pa, bp), slot(pa, bp), near + 8, sib)
    hidden_chunk(1)
    landed(slot(a2, pb).at[top], base + 2)
    landed(slot(a2, pb).at[bottom], base + 3)
    send(slot(a2, pb), slot(a2, pb), base + 16, to_bp)
    send(slot(a2, pb), slot(a2, pb), base + 17, to_bm)
    send(slot(a2, pb), slot(a2, pb), near + 3, sib)
    for j in (1, 2, 3):
        a = columns[j]
        landed(slot(a, bm), base + 4 + 4 * j)
        send(slot(a, bm).at[top], slot(a, bm).at[top], base + 6 + 4 * j, to_bp)
        send(slot(a, bm), slot(a, bm), near + 4 + j, sib)
        landed(slot(a, bp), base + 5 + 4 * j)
        send(slot(a, bp).at[bottom], slot(a, bp).at[bottom], base + 7 + 4 * j, to_bm)
        send(slot(a, bp), slot(a, bp), near + 8 + j, sib)
        if j < 3:
            hidden_chunk(1 + j)
    for j in (0, 1, 2, 3):
        a = columns[j]
        landed(slot(a, b2).at[top], base + 6 + 4 * j)
        landed(slot(a, b2).at[bottom], base + 7 + 4 * j)
        send(slot(a, b2), slot(a, b2), near + 12 + j, sib)
    for i in range(16):
        landed(wl.at[0], near + i)
    own.wait()

    place = lax.broadcasted_iota(jnp.int32, (SB, LB), 1)

    def block(b, carry):
        wanted = pos[b]
        for k in range(BEAM):
            c = sl[b * BEAM + k]
            for j in range(D // LB):
                w4[k * LB:(k + 1) * LB, j * LB:(j + 1) * LB] = wl[c, j * LB:(j + 1) * LB, :]
        rows = hid[b]
        parts = []
        for k in range(BEAM):
            c = sl[b * BEAM + k]
            tail = wl[c, D:SHARD, :].astype(F32)
            scale = tail[0:1] / tail[1:2]
            logits = lax.dot_general(
                rows, w4[k * LB:(k + 1) * LB, :], (((1,), (1,)), ((), ())),
                preferred_element_type=F32,
            )
            hit = wanted[:, 0:1] == place + k * LB
            for column in range(1, wanted.shape[1]):
                hit = hit | (wanted[:, column:column + 1] == place + k * LB)
            target = jnp.where(hit, 1.0, 0.0)
            part = (scale * (jax.nn.sigmoid(logits) - target) / SB).astype(BF16)
            gl[b * BEAM + k] = part
            parts.append(part)
        total = jnp.dot(jnp.concatenate(parts, axis=1), w4[...], preferred_element_type=F32)
        gh[pl.ds(pl.multiple_of(b * SB, SB), SB), :] = total.astype(BF16)
        return carry

    lax.fori_loop(0, NBLK, block, 0)

    def proj_half(which):
        lanes = pl.ds(pl.multiple_of(which * (D // 2), 128), D // 2)
        return jnp.dot(enct[...], gh[:, lanes], preferred_element_type=F32)

    value = proj_half(other)
    for j in range(3):
        ps0[j * D:(j + 1) * D, :] = value[:, j * LB:(j + 1) * LB].astype(BF16)

    def cluster(c):
        left = jnp.concatenate([hidt[tab[1, c]], hidt[tab[3, c]]], axis=1)
        one = (gl[tab[0, c]].astype(F32) * live[0, c]).astype(BF16)
        two = (gl[tab[2, c]].astype(F32) * live[1, c]).astype(BF16)
        return jnp.dot(left, jnp.concatenate([one, two], axis=0), preferred_element_type=F32)

    pair0 = take()
    value = proj_half(core)
    send(ps0, pr0, pair0, sib)
    for j in range(3):
        pf[j * D:(j + 1) * D, :] = value[:, j * LB:(j + 1) * LB]

    cross = take(16)

    def across(i):
        return remote(sb.at[i], rb.at[i], cross + i, sib)

    def for_other(i, carry):
        c = lid((pb + 6 - i // 4) % 4, (pa + 6 - i % 4) % 4, other)
        sb[i] = cluster(c).astype(BF16)

        @pl.when(i > 0)
        def _():
            across(i - 1).start()

        return carry

    lax.fori_loop(0, 16, for_other, 0)
    landed(pr0, pair0)
    pf[...] = pf[...] + pr0[...].astype(F32)
    across(15).start()

    def ablk(a):
        return pl.ds(pl.multiple_of(a * ABLK, 16), ABLK)

    pa1[...] = pf[ablk(a2), :].astype(BF16)

    def own_cluster(da, db):
        c = lid((pa + 6 - da) % 4, (pb + 6 - db) % 4, core)
        i = da * 4 + db
        value = cluster(c)
        across(i).wait_recv()
        return value + rb[i].astype(F32)

    def far(db, carry):
        cb[db] = own_cluster(0, db).astype(BF16)
        return carry

    lax.fori_loop(0, 4, far, 0)
    pm1 = take(2)
    send(pa1.at[pl.ds(0, ABLK // 2)], p1a, pm1, to_ap)
    send(pa1.at[pl.ds(ABLK // 2, ABLK // 2)], p1b, pm1 + 1, to_am)

    def nearby(i, carry):
        cf[i] = own_cluster(1 + i // 4, i % 4)
        return carry

    lax.fori_loop(0, 4, nearby, 0)
    m1 = take(8)
    upper, lower = pl.ds(0, D // 2), pl.ds(D // 2, D // 2)
    for db in range(4):
        send(cb.at[db, upper], r1a.at[db], m1 + db, to_ap)
        send(cb.at[db, lower], r1b.at[db], m1 + 4 + db, to_am)
    lax.fori_loop(4, 12, nearby, 0)

    outs = []

    def enc_chunk(i):
        rows = pl.ds(256 * i, 256)
        ge[rows, :] = lax.dot_general(
            gh[rows, :], proj[...], (((1,), (1,)), ((), ())), preferred_element_type=F32
        )
        if i > 0:
            out_chunk(i - 1)

    def out_chunk(i):
        rows = pl.ds(256 * i, 256)
        copy = pltpu.make_async_copy(ge.at[rows], ge_out.at[rows], ls.at[1 + i])
        copy.start()
        outs.append(copy)

    landed(p1a, pm1)
    landed(p1b, pm1 + 1)
    half = ABLK // 2
    up = pf[ablk(ap), :]
    ps2p[0:half, :] = (up[0:half] + p1a[...].astype(F32)).astype(BF16)
    ps2p[half:, :] = up[half:].astype(BF16)
    down = pf[ablk(am), :]
    ps2m[0:half, :] = down[0:half].astype(BF16)
    ps2m[half:, :] = (down[half:] + p1b[...].astype(F32)).astype(BF16)
    m2 = take(8)
    pm2 = take(2)
    for db in range(4):
        landed(r1a.at[db], m1 + db)
        landed(r1b.at[db], m1 + 4 + db)
        s2p[db, 0:384, :] = (cf[db, 0:384, :] + r1a[db].astype(F32)).astype(BF16)
        s2p[db, 384:768, :] = cf[db, 384:768, :].astype(BF16)
        s2m[db, 0:384, :] = cf[8 + db, 0:384, :].astype(BF16)
        s2m[db, 384:768, :] = (cf[8 + db, 384:768, :] + r1b[db].astype(F32)).astype(BF16)
        if db == 0:
            send(ps2p, pr2p, pm2, to_ap)
            send(ps2m, pr2m, pm2 + 1, to_am)
        else:
            send(s2p.at[db - 1], r2p.at[db - 1], m2 + db - 1, to_ap)
            send(s2m.at[db - 1], r2m.at[db - 1], m2 + 4 + db - 1, to_am)
    enc_chunk(0)
    send(s2p.at[3], r2p.at[3], m2 + 3, to_ap)
    send(s2m.at[3], r2m.at[3], m2 + 7, to_am)
    landed(pr2p, pm2)
    landed(pr2m, pm2 + 1)
    mine = ablk(pa)
    pf[mine, :] = pf[mine, :] + pr2p[...].astype(F32) + pr2m[...].astype(F32)

    def piece(b):
        return pl.ds(pl.multiple_of(pa * ABLK + b * PIECE, 16), PIECE)

    pb0[...] = pf[piece(b2), :].astype(BF16)
    n1 = take(2)
    pn1 = take(2)
    n2 = take(2)
    pn2 = take(2)
    cut = 80

    def finish_a(db):
        landed(r2p.at[db], m2 + db)
        landed(r2m.at[db], m2 + 4 + db)
        return cf[4 + db] + r2p[db].astype(F32) + r2m[db].astype(F32)

    db0[...] = finish_a(0).astype(BF16)
    send(pb0.at[pl.ds(0, cut)], q1a, pn1, to_bp)
    send(pb0.at[pl.ds(cut, PIECE - cut)], q1b, pn1 + 1, to_bm)
    cf[5] = finish_a(1)
    send(db0.at[upper], t1a, n1, to_bp)
    send(db0.at[lower], t1b, n1 + 1, to_bm)
    cf[6] = finish_a(2)
    cf[7] = finish_a(3)
    landed(q1a, pn1)
    landed(q1b, pn1 + 1)
    up = pf[piece(bp), :]
    qs2p[0:cut, :] = (up[0:cut] + q1a[...].astype(F32)).astype(BF16)
    qs2p[cut:, :] = up[cut:].astype(BF16)
    down = pf[piece(bm), :]
    qs2m[0:cut, :] = down[0:cut].astype(BF16)
    qs2m[cut:, :] = (down[cut:] + q1b[...].astype(F32)).astype(BF16)
    landed(t1a, n1)
    landed(t1b, n1 + 1)
    u2p[0:384, :] = (cf[5, 0:384, :] + t1a[...].astype(F32)).astype(BF16)
    u2p[384:768, :] = cf[5, 384:768, :].astype(BF16)
    send(qs2p, qr2p, pn2, to_bp)
    send(qs2m, qr2m, pn2 + 1, to_bm)
    u2m[0:384, :] = cf[7, 0:384, :].astype(BF16)
    u2m[384:768, :] = (cf[7, 384:768, :] + t1b[...].astype(F32)).astype(BF16)
    enc_chunk(1)
    send(u2p, v2p, n2, to_bp)
    send(u2m, v2m, n2 + 1, to_bm)
    landed(qr2p, pn2)
    landed(qr2m, pn2 + 1)
    value = pf[piece(pb), :] + qr2p[...].astype(F32) + qr2m[...].astype(F32)
    ez[...] = value.astype(BF16)
    zp[z] = value.astype(BF16)
    pz = take(NZ)
    landed(v2p, n2)
    landed(v2m, n2 + 1)
    for dz in (4, 3, 5, 2, 6, 1, 7):
        send(ez, zp.at[z], pz + dz, to_z[dz])
    value = cf[6] + v2p[...].astype(F32) + v2m[...].astype(F32)
    value = value.reshape(NZ, D // NZ, LB)
    ef[...] = value
    zs[...] = value.astype(BF16)
    hz = take(NZ)
    enc_chunk(2)
    for dz in (4, 3, 5, 2, 6, 1, 7):
        send(zs.at[(z + dz) % NZ], zr.at[dz], hz + dz, to_z[dz])
    for dz in range(1, NZ):
        landed(zp.at[(z + NZ - dz) % NZ], pz + dz)
    total = zp[0].astype(F32)
    for i in range(1, NZ):
        total = total + zp[i].astype(F32)

    def spot(a, b):
        return pl.ds(pl.multiple_of((core * 4 + a) * ABLK + b * PIECE, 16), PIECE)

    def part(a, b, start, size):
        return pl.ds(pl.multiple_of((core * 4 + a) * ABLK + b * PIECE + start, 16), size)

    po[spot(pa, pb), :] = total.astype(BF16)
    g1 = take(4)
    enc_chunk(3)
    send(po.at[spot(pa, pb)], po.at[spot(pa, pb)], g1, to_bp)
    send(po.at[spot(pa, pb)], po.at[spot(pa, pb)], g1 + 1, to_bm)
    out_chunk(3)
    for dz in range(1, NZ):
        landed(zr.at[dz], hz + dz)
    value = ef[z]
    for dz in range(1, NZ):
        value = value + zr[dz].astype(F32)
    gh_out[...] = value
    landed(po.at[spot(pa, bm)], g1)
    send(po.at[part(pa, bm, 0, cut)], po.at[part(pa, bm, 0, cut)], g1 + 2, to_bp)
    landed(po.at[spot(pa, bp)], g1 + 1)
    send(po.at[part(pa, bp, cut, PIECE - cut)], po.at[part(pa, bp, cut, PIECE - cut)], g1 + 3, to_bm)
    landed(po.at[part(pa, b2, 0, cut)], g1 + 2)
    landed(po.at[part(pa, b2, cut, PIECE - cut)], g1 + 3)

    def wide(a, start, size):
        return pl.ds(pl.multiple_of((core * 4 + a) * ABLK + start, 16), size)

    g2 = take(4)
    g3 = take(4)
    row = po.at[wide(pa, 0, ABLK)]
    send(row, row, g2, to_ap)
    send(row, row, g2 + 1, to_am)
    send(row, row, g3, sib)
    row = po.at[wide(am, 0, ABLK)]
    landed(row, g2)
    send(po.at[wide(am, 0, half)], po.at[wide(am, 0, half)], g2 + 2, to_ap)
    send(row, row, g3 + 1, sib)
    row = po.at[wide(ap, 0, ABLK)]
    landed(row, g2 + 1)
    send(po.at[wide(ap, half, half)], po.at[wide(ap, half, half)], g2 + 3, to_am)
    send(row, row, g3 + 2, sib)
    row = po.at[wide(a2, 0, ABLK)]
    landed(po.at[wide(a2, 0, half)], g2 + 2)
    landed(po.at[wide(a2, half, half)], g2 + 3)
    send(row, row, g3 + 3, sib)
    for i in range(4):
        landed(row, g3 + i)
    last = pltpu.make_async_copy(po, gp_out, ls.at[5])
    last.start()
    for copy in sent:
        copy.wait_send()

    def drain(i, carry):
        across(i).wait_send()
        return carry

    lax.fori_loop(0, 16, drain, 0)
    for copy in outs:
        copy.wait()
    last.wait()
    assert count[0] <= MESSAGES, count[0]


MESSAGES = 128


def scratch():
    v = pltpu.VMEM
    return [
        v((32, SHARD, LB), BF16), v((NBLK, SB, D), BF16), v((NBLK, D, SB), BF16),
        v((D, ROWS), BF16), v((BEAM * LB, D), BF16), v((32, SB, LB), BF16),
        v((ROWS, D), BF16), v((ROWS, D), F32),
        v((16, D, LB), BF16), v((16, D, LB), BF16), v((4, D, LB), BF16), v((12, D, LB), F32),
        v((4, D // 2, LB), BF16), v((4, D // 2, LB), BF16),
        v((4, D, LB), BF16), v((4, D, LB), BF16), v((4, D, LB), BF16), v((4, D, LB), BF16),
        v((D, LB), BF16), v((D // 2, LB), BF16), v((D // 2, LB), BF16),
        v((D, LB), BF16), v((D, LB), BF16), v((D, LB), BF16), v((D, LB), BF16),
        v((NZ, D // NZ, LB), F32), v((NZ, D // NZ, LB), BF16), v((NZ, D // NZ, LB), BF16),
        v((CORE, LB), BF16), v((CORE, LB), BF16), v((CORE, LB), F32),
        v((ABLK, LB), BF16), v((ABLK // 2, LB), BF16), v((ABLK // 2, LB), BF16),
        v((ABLK, LB), BF16), v((ABLK, LB), BF16), v((ABLK, LB), BF16), v((ABLK, LB), BF16),
        v((PIECE, LB), BF16), v((80, LB), BF16), v((PIECE - 80, LB), BF16),
        v((PIECE, LB), BF16), v((PIECE, LB), BF16), v((PIECE, LB), BF16), v((PIECE, LB), BF16),
        v((PIECE, LB), BF16), v((NZ, PIECE, LB), BF16), v((2 * CORE, LB), BF16),
        pltpu.SemaphoreType.DMA((MESSAGES,)), pltpu.SemaphoreType.DMA((MESSAGES,)),
        pltpu.SemaphoreType.DMA((8,)),
    ]


def shards(enc, proj, head_weight, shortlist, positives, weight_num, weight_den):
    size = head_weight.shape[0]
    flat = shortlist.reshape(-1)
    pairs = flat.shape[0]
    match = flat[None, :] == jnp.arange(32, dtype=jnp.int32)[:, None]
    order = jnp.arange(pairs, dtype=jnp.int32)[None, :]
    total = jnp.sum(match.astype(jnp.int32), axis=1)
    one = jnp.min(jnp.where(match, order, pairs - 1), axis=1)
    two = jnp.max(jnp.where(match, order, 0), axis=1)
    tab = jnp.stack([one, one // BEAM, two, two // BEAM])
    live = jnp.stack([total > 0, total > 1]).astype(F32)
    tail = jnp.zeros((16, LB), BF16)
    tail = tail.at[0].set(weight_num.astype(BF16)).at[1].set(weight_den.astype(BF16))
    tail = tail.at[2:].set(1)
    shard = jnp.concatenate(
        [head_weight.reshape(size, D // LB, LB).transpose(1, 0, 2).reshape(D, LB), tail], axis=0
    )
    smem = pl.BlockSpec(memory_space=pltpu.SMEM)
    vmem = pl.BlockSpec(memory_space=pltpu.VMEM)
    anyspace = pl.BlockSpec(memory_space=pl.ANY)
    grad_enc, grad_proj, grad_head = pl.pallas_call(
        kernel,
        out_shape=(
            jax.ShapeDtypeStruct((ROWS, D), F32),
            jax.ShapeDtypeStruct((2 * CORE, LB), BF16),
            jax.ShapeDtypeStruct((D // NZ, LB), F32),
        ),
        in_specs=[smem, smem, smem, vmem, vmem, vmem, vmem],
        out_specs=(anyspace, anyspace, vmem),
        scratch_shapes=scratch(),
        compiler_params=pltpu.CompilerParams(
            collective_id=0, has_side_effects=True, vmem_limit_bytes=62 << 20
        ),
    )(flat, tab, live, enc, proj, shard, positives.reshape(NBLK, SB, -1))
    grad_proj = grad_proj.reshape(D // LB, D, LB).transpose(1, 0, 2).reshape(D, D).astype(F32)
    return (grad_enc, grad_proj, grad_head.T)


def solution(mesh):
    placed = (
        P(("dp", "label"), None),
        P(),
        P("label", None),
        P(("dp", "label"), None),
        P(("dp", "label"), None),
        P("label"),
        P("label"),
    )
    return jax.shard_map(
        shards,
        mesh=mesh,
        in_specs=placed,
        out_specs=(P(("dp", "label"), None), P(), P("label", "dp")),
        check_vma=False,
    )
```

```python
import jax
import jax.numpy as jnp
from jax import lax
from jax.experimental import pallas as pl
from jax.experimental.pallas import tpu as pltpu
from jax.sharding import PartitionSpec as P

MESH = pl.DeviceIdType.MESH
F32 = jnp.float32
BF16 = jnp.bfloat16

D = 768
LB = 128
SB = 128
BEAM = 4
NBLK = 8
ROWS = NBLK * SB
SHARD = D + 16
HALF0, HALF1 = 400, 384
NZ = 8
PIECE = 144
ABLK = 4 * PIECE
CORE = 4 * ABLK


def lid(pa, pb, core):
    xx = pa + core * (pb - pa)
    yy = pb + core * (pa - pb)
    return (yy * 4 + xx) * 2 + core


def kernel(
    sl, tab, num, den, post, enc_in, proj_in, head_in,
    ge_out, gp_out, gh_out,
    enc, proj, wl, pos, hid, hidt, enct, w4, gl, gh, ge,
    sb, rb, cb, cf, ra, dbs, rbb, ef, zs, zr,
    ps0, pr0, pf, pas, pra, pbs, prb, ez, zp, po,
    ss, rs, ls,
):
    z = lax.axis_index("dp")
    me = lax.axis_index("label")
    core = me % 2
    x = (me // 2) % 4
    y = me // 8
    pa = x + core * (y - x)
    pb = y + core * (x - y)
    other = 1 - core
    ap, am, a2 = (pa + 1) % 4, (pa + 3) % 4, (pa + 2) % 4
    bp, bm, b2 = (pb + 1) % 4, (pb + 3) % 4, (pb + 2) % 4
    sib = {"label": me + 1 - 2 * core}
    to_ap = {"label": lid(ap, pb, core)}
    to_am = {"label": lid(am, pb, core)}
    to_a2 = {"label": lid(a2, pb, core)}
    to_bp = {"label": lid(pa, bp, core)}
    to_bm = {"label": lid(pa, bm, core)}
    to_b2 = {"label": lid(pa, b2, core)}
    to_z = [None] + [{"dp": (z + dz) % NZ} for dz in range(1, NZ)]

    barrier = pltpu.get_barrier_semaphore()
    greeted = [sib, to_ap, to_am, to_a2, to_bp, to_bm, to_b2] + to_z[1:]
    for device in greeted:
        pl.semaphore_signal(barrier, inc=1, device_id=device, device_id_type=MESH)

    loads = []
    for j in range(D // LB):
        loads.append(pltpu.make_async_copy(
            head_in.at[:, pl.ds(j * LB, LB)], wl.at[me, pl.ds(j * LB, LB)], ls.at[j]))
    loads.append(pltpu.make_async_copy(proj_in, proj, ls.at[6]))
    loads.append(pltpu.make_async_copy(enc_in, enc, ls.at[7]))
    for load in loads:
        load.start()
    line = lax.broadcasted_iota(jnp.int32, (16, LB), 0)
    tail = jnp.where(line == 0, num[...], jnp.where(line == 1, den[...], 1))
    wl[me, D:SHARD, :] = tail.astype(F32).astype(BF16)

    count = [0]
    sent = []

    def take(n=1):
        first = count[0]
        count[0] += n
        return first

    def remote(src, dst, i, device):
        return pltpu.make_async_remote_copy(
            src_ref=src, dst_ref=dst, send_sem=ss.at[i], recv_sem=rs.at[i],
            device_id=device, device_id_type=MESH,
        )

    def send(src, dst, i, device):
        copy = remote(src, dst, i, device)
        copy.start()
        sent.append(copy)

    def landed(dst, i):
        remote(dst, dst, i, sib).wait_recv()

    def hidden_chunk(i):
        for b in (2 * i, 2 * i + 1):
            pos[b] = post[:, b * SB:(b + 1) * SB].T
        rows = enc[pl.ds(256 * i, 256), :]
        value = jnp.dot(rows, proj[...], preferred_element_type=F32).astype(BF16)
        hid[2 * i] = value[:SB]
        hid[2 * i + 1] = value[SB:]
        hidt[2 * i] = value[:SB].T
        hidt[2 * i + 1] = value[SB:].T
        enct[:, pl.ds(256 * i, 256)] = rows.T

    for load in loads[:6]:
        load.wait()
    pl.semaphore_wait(barrier, len(greeted))
    top, bottom = pl.ds(0, HALF0), pl.ds(HALF0, HALF1)
    first = take(3)
    base = take(16)
    near = take(16)

    def slot(a, b):
        return wl.at[lid(a, b, core)]

    columns = [pa, am, ap, a2]
    own = wl.at[me]
    early = [remote(own, own, first, to_ap), remote(own, own, first + 1, to_am)]
    for copy in early:
        copy.start()
    send(own, own, first + 2, to_a2)
    send(own, own, near, sib)
    for copy in early:
        copy.wait_send()
    send(own, own, base, to_bp)
    send(own, own, base + 1, to_bm)
    loads[6].wait()
    loads[7].wait()
    hidden_chunk(0)

    def spread(j):
        held = slot(columns[j], pb)
        send(held, held, base + 4 * j, to_bp)
        send(held, held, base + 4 * j + 1, to_bm)
        send(held, held, near + j, sib)

    def forward(j):
        a = columns[j]
        held = slot(a, bm)
        landed(held, base + 4 * j)
        send(held.at[top], held.at[top], base + 4 * j + 2, to_bp)
        send(held, held, near + 4 + j, sib)
        held = slot(a, bp)
        landed(held, base + 4 * j + 1)
        send(held.at[bottom], held.at[bottom], base + 4 * j + 3, to_bm)
        send(held, held, near + 8 + j, sib)

    landed(slot(am, pb), first)
    spread(1)
    landed(slot(ap, pb), first + 1)
    spread(2)
    forward(0)
    landed(slot(a2, pb), first + 2)
    spread(3)
    hidden_chunk(1)
    forward(1)
    hidden_chunk(2)
    forward(2)
    hidden_chunk(3)
    forward(3)
    for j in (0, 1, 2, 3):
        held = slot(columns[j], b2)
        landed(held.at[top], base + 4 * j + 2)
        landed(held.at[bottom], base + 4 * j + 3)
        send(held, held, near + 12 + j, sib)
    for i in range(16):
        landed(own, near + i)

    place = lax.broadcasted_iota(jnp.int32, (SB, LB), 1)

    def block(b, carry):
        wanted = pos[b]
        for k in range(BEAM):
            c = sl[k, b]
            for j in range(D // LB):
                w4[k * LB:(k + 1) * LB, j * LB:(j + 1) * LB] = wl[c, j * LB:(j + 1) * LB, :]
        rows = hid[b]
        parts = []
        for k in range(BEAM):
            c = sl[k, b]
            ends = wl[c, D:SHARD, :].astype(F32)
            scale = ends[0:1] / ends[1:2]
            logits = lax.dot_general(
                rows, w4[k * LB:(k + 1) * LB, :], (((1,), (1,)), ((), ())),
                preferred_element_type=F32,
            )
            hit = wanted[:, 0:1] == place + k * LB
            for column in range(1, wanted.shape[1]):
                hit = hit | (wanted[:, column:column + 1] == place + k * LB)
            target = jnp.where(hit, 1.0, 0.0)
            part = (scale * (jax.nn.sigmoid(logits) - target) / SB).astype(BF16)
            gl[b * BEAM + k] = part
            parts.append(part)
        total = jnp.dot(jnp.concatenate(parts, axis=1), w4[...], preferred_element_type=F32)
        gh[pl.ds(pl.multiple_of(b * SB, SB), SB), :] = total.astype(BF16)
        return carry

    lax.fori_loop(0, NBLK, block, 0)

    def proj_half(which):
        lanes = pl.ds(pl.multiple_of(which * (D // 2), 128), D // 2)
        return jnp.dot(enct[...], gh[:, lanes], preferred_element_type=F32)

    value = proj_half(other)
    for j in range(3):
        ps0[j * D:(j + 1) * D, :] = value[:, j * LB:(j + 1) * LB].astype(BF16)
    value = proj_half(core)
    pair0 = take()
    send(ps0, pr0, pair0, sib)
    for j in range(3):
        pf[j * D:(j + 1) * D, :] = value[:, j * LB:(j + 1) * LB]

    def cluster(c):
        code = tab[c]
        one = lax.rem(code, 32)
        two = lax.rem(lax.div(code, 32), 32)
        total = lax.div(code, 1024)
        left = jnp.concatenate([hidt[lax.div(one, BEAM)], hidt[lax.div(two, BEAM)]], axis=1)
        up = gl[one].astype(F32) * jnp.minimum(total, 1).astype(F32)
        down = gl[two].astype(F32) * jnp.maximum(total - 1, 0).astype(F32)
        right = jnp.concatenate([up.astype(BF16), down.astype(BF16)], axis=0)
        return jnp.dot(left, right, preferred_element_type=F32)

    cross = take(16)

    def across(i):
        return remote(sb.at[i], rb.at[i], cross + i, sib)

    def for_other(i, carry):
        c = lid((pb + 6 - i % 4) % 4, (pa + 6 - i // 4) % 4, other)
        sb[i] = cluster(c).astype(BF16)

        @pl.when(i > 0)
        def _():
            across(i - 1).start()

        return carry

    lax.fori_loop(0, 16, for_other, 0)

    def ablk(a):
        return pl.ds(pl.multiple_of(a * ABLK, 16), ABLK)

    landed(pr0, pair0)
    across(15).start()
    pm = take(3)

    def pack(r, a):
        pas[r] = (pf[ablk(a), :] + pr0[ablk(a), :].astype(F32)).astype(BF16)

    pack(2, a2)
    pack(0, ap)
    send(pas.at[2], pra.at[2], pm + 2, to_a2)
    pack(1, am)
    send(pas.at[0], pra.at[0], pm, to_ap)
    mine = ablk(pa)
    pf[mine, :] = pf[mine, :] + pr0[mine, :].astype(F32)
    send(pas.at[1], pra.at[1], pm + 1, to_am)

    hm = take(12)

    def along_a(db, r):
        return remote(cb.at[db * 3 + r], ra.at[r, db], hm + db * 3 + r, (to_ap, to_am, to_a2)[r])

    def own_clusters(db, carry):
        def value_of(da):
            c = lid((pa + 6 - da) % 4, (pb + 6 - db) % 4, core)
            value = cluster(c)
            across(db * 4 + da).wait_recv()
            return value + rb[db * 4 + da].astype(F32)

        cb[db * 3 + 2] = value_of(0).astype(BF16)
        cb[db * 3] = value_of(1).astype(BF16)
        along_a(db, 2).start()
        cb[db * 3 + 1] = value_of(3).astype(BF16)
        along_a(db, 0).start()
        cf[db] = value_of(2)
        along_a(db, 1).start()
        return carry

    lax.fori_loop(0, 4, own_clusters, 0)

    outs = []

    def enc_chunk(i):
        rows = pl.ds(256 * i, 256)
        ge[rows, :] = lax.dot_general(
            gh[rows, :], proj[...], (((1,), (1,)), ((), ())), preferred_element_type=F32
        )
        if i > 0:
            out_chunk(i - 1)

    def out_chunk(i):
        rows = pl.ds(256 * i, 256)
        copy = pltpu.make_async_copy(ge.at[rows], ge_out.at[rows], ls.at[8 + i])
        copy.start()
        outs.append(copy)

    enc_chunk(0)
    for r in range(3):
        landed(pra.at[r], pm + r)
    value = pf[mine, :] + pra[0].astype(F32) + pra[1].astype(F32) + pra[2].astype(F32)
    pf[mine, :] = value
    pbs[...] = value.astype(BF16)

    def piece(b):
        return pl.ds(pl.multiple_of(b * PIECE, 16), PIECE)

    pn = take(3)
    enc_chunk(1)
    send(pbs.at[piece(b2)], prb.at[2], pn + 2, to_b2)
    send(pbs.at[piece(bp)], prb.at[0], pn, to_bp)
    send(pbs.at[piece(bm)], prb.at[1], pn + 1, to_bm)
    hn = take(3)

    def finish_a(db):
        for r in range(3):
            landed(ra.at[r, db], hm + db * 3 + r)
        return cf[db] + ra[0, db].astype(F32) + ra[1, db].astype(F32) + ra[2, db].astype(F32)

    dbs[2] = finish_a(0).astype(BF16)
    for r in range(3):
        landed(prb.at[r], pn + r)
    spot_rows = pl.ds(pl.multiple_of(pa * ABLK + pb * PIECE, 16), PIECE)
    value = pf[spot_rows, :] + prb[0].astype(F32) + prb[1].astype(F32) + prb[2].astype(F32)
    ez[...] = value.astype(BF16)
    zp[z] = value.astype(BF16)
    pz = take(NZ)
    send(dbs.at[2], rbb.at[2], hn + 2, to_b2)
    enc_chunk(2)
    for dz in (4, 3, 5, 2, 6, 1, 7):
        send(ez, zp.at[z], pz + dz, to_z[dz])
    dbs[0] = finish_a(1).astype(BF16)
    enc_chunk(3)
    send(dbs.at[0], rbb.at[0], hn, to_bp)
    out_chunk(3)
    cf[2] = finish_a(2)
    dbs[1] = finish_a(3).astype(BF16)
    for dz in range(1, NZ):
        landed(zp.at[(z + NZ - dz) % NZ], pz + dz)
    send(dbs.at[1], rbb.at[1], hn + 1, to_bm)
    total = zp[0].astype(F32)
    for i in range(1, NZ):
        total = total + zp[i].astype(F32)

    def spot(a, b):
        return po.at[pl.ds(pl.multiple_of((core * 4 + a) * ABLK + b * PIECE, 16), PIECE)]

    def wide(a):
        return po.at[pl.ds(pl.multiple_of((core * 4 + a) * ABLK, 16), ABLK)]

    po[pl.ds(pl.multiple_of((core * 4 + pa) * ABLK + pb * PIECE, 16), PIECE), :] = total.astype(BF16)
    g1 = take(3)
    landed(rbb.at[2], hn + 2)
    landed(rbb.at[0], hn)
    for r, device in enumerate((to_bp, to_bm, to_b2)):
        send(spot(pa, pb), spot(pa, pb), g1 + r, device)
    landed(rbb.at[1], hn + 1)
    value = cf[2] + rbb[0].astype(F32) + rbb[1].astype(F32) + rbb[2].astype(F32)
    value = value.reshape(NZ, D // NZ, LB)
    ef[...] = value
    zs[...] = value.astype(BF16)
    hz = take(NZ)
    landed(spot(pa, bm), g1)
    for dz in (4, 3, 5, 2, 6, 1, 7):
        send(zs.at[(z + dz) % NZ], zr.at[dz], hz + dz, to_z[dz])
    landed(spot(pa, bp), g1 + 1)
    landed(spot(pa, b2), g1 + 2)
    g2 = take(3)
    g3 = take(4)
    for r, device in enumerate((to_ap, to_am, to_a2)):
        send(wide(pa), wide(pa), g2 + r, device)
    send(wide(pa), wide(pa), g3, sib)
    for r, a in enumerate((am, ap, a2)):
        landed(wide(a), g2 + r)
        send(wide(a), wide(a), g3 + 1 + r, sib)
    for dz in range(1, NZ):
        landed(zr.at[dz], hz + dz)
    value = ef[z]
    for dz in range(1, NZ):
        value = value + zr[dz].astype(F32)
    gh_out[...] = value
    for i in range(4):
        landed(wide(pa), g3 + i)
    for j in range(D // LB):
        copy = pltpu.make_async_copy(
            po.at[pl.ds(j * D, D)], gp_out.at[:, pl.ds(j * LB, LB)], ls.at[j])
        copy.start()
        outs.append(copy)
    for copy in sent:
        copy.wait_send()

    def drain(i, carry):
        across(i).wait_send()
        return carry

    lax.fori_loop(0, 16, drain, 0)

    def drain_a(db, carry):
        for r in range(3):
            along_a(db, r).wait_send()
        return carry

    lax.fori_loop(0, 4, drain_a, 0)
    for copy in outs:
        copy.wait()
    assert count[0] <= MESSAGES, count[0]


MESSAGES = 128


def scratch():
    v = pltpu.VMEM
    return [
        v((ROWS, D), BF16), v((D, D), BF16),
        v((32, SHARD, LB), BF16), v((NBLK, SB, 8), jnp.int32),
        v((NBLK, SB, D), BF16), v((NBLK, D, SB), BF16),
        v((D, ROWS), BF16), v((BEAM * LB, D), BF16), v((32, SB, LB), BF16),
        v((ROWS, D), BF16), v((ROWS, D), F32),
        v((16, D, LB), BF16), v((16, D, LB), BF16), v((12, D, LB), BF16), v((4, D, LB), F32),
        v((3, 4, D, LB), BF16), v((3, D, LB), BF16), v((3, D, LB), BF16),
        v((NZ, D // NZ, LB), F32), v((NZ, D // NZ, LB), BF16), v((NZ, D // NZ, LB), BF16),
        v((CORE, LB), BF16), v((CORE, LB), BF16), v((CORE, LB), F32),
        v((3, ABLK, LB), BF16), v((3, ABLK, LB), BF16),
        v((ABLK, LB), BF16), v((3, PIECE, LB), BF16),
        v((PIECE, LB), BF16), v((NZ, PIECE, LB), BF16), v((2 * CORE, LB), BF16),
        pltpu.SemaphoreType.DMA((MESSAGES,)), pltpu.SemaphoreType.DMA((MESSAGES,)),
        pltpu.SemaphoreType.DMA((12,)),
    ]


def shards(enc, proj, head_weight, shortlist, positives, weight_num, weight_den):
    ids = jnp.arange(32, dtype=jnp.int32)[:, None, None]
    match = shortlist[None] == ids
    order = jnp.arange(NBLK * BEAM, dtype=jnp.int32).reshape(1, NBLK, BEAM)
    total = jnp.sum(match.astype(jnp.int32), axis=(1, 2))
    one = jnp.min(jnp.where(match, order, NBLK * BEAM - 1), axis=(1, 2))
    two = jnp.max(jnp.where(match, order, 0), axis=(1, 2))
    tab = one + 32 * two + 1024 * total
    smem = pl.BlockSpec(memory_space=pltpu.SMEM)
    vmem = pl.BlockSpec(memory_space=pltpu.VMEM)
    anyspace = pl.BlockSpec(memory_space=pl.ANY)
    grad_enc, grad_proj, grad_head = pl.pallas_call(
        kernel,
        out_shape=(
            jax.ShapeDtypeStruct((ROWS, D), F32),
            jax.ShapeDtypeStruct((D, D), BF16),
            jax.ShapeDtypeStruct((D // NZ, LB), F32),
        ),
        in_specs=[smem, smem, vmem, vmem, vmem, anyspace, anyspace, anyspace],
        out_specs=(anyspace, anyspace, vmem),
        scratch_shapes=scratch(),
        compiler_params=pltpu.CompilerParams(
            collective_id=0, has_side_effects=True, vmem_limit_bytes=60 << 20
        ),
    )(
        shortlist.T, tab, weight_num.reshape(1, LB), weight_den.reshape(1, LB), positives.T,
        enc, proj, head_weight,
    )
    return (grad_enc, grad_proj.astype(F32), grad_head.T)


def solution(mesh):
    placed = (
        P(("dp", "label"), None),
        P(),
        P("label", None),
        P(("dp", "label"), None),
        P(("dp", "label"), None),
        P("label"),
        P("label"),
    )
    return jax.shard_map(
        shards,
        mesh=mesh,
        in_specs=placed,
        out_specs=(P(("dp", "label"), None), P(), P("label", "dp")),
        check_vma=False,
    )
```

```python
import jax
import jax.numpy as jnp
from jax import lax
from jax.experimental import pallas as pl
from jax.experimental.pallas import tpu as pltpu
from jax.sharding import PartitionSpec as P

MESH = pl.DeviceIdType.MESH
F32 = jnp.float32
BF16 = jnp.bfloat16

D = 768
LB = 128
SB = 128
BEAM = 4
NBLK = 8
ROWS = NBLK * SB
SHARD = D + 16
HALF0, HALF1 = 400, 384
NZ = 8
PIECE = 144
ABLK = 4 * PIECE
CORE = 4 * ABLK


def lid(pa, pb, core):
    xx = pa + core * (pb - pa)
    yy = pb + core * (pa - pb)
    return (yy * 4 + xx) * 2 + core


def kernel(
    sl, tab, num_in, den_in, post_in, enc_in, proj_in, head_in,
    ge, gp_out, gh_out,
    num, den, post, enc, proj, wl, pos, hid, hidt, hidt_s, enct, enct_s, w4, gl, gl_s, gh, gh_s,
    cb, cf, ra, dbs, rbb, ef, zs, zr,
    pf, pas, pra, pbs, prb, ez, zp, po, tab_s,
    ss, rs, ls,
):
    z = lax.axis_index("dp")
    me = lax.axis_index("label")
    core = me % 2
    x = (me // 2) % 4
    y = me // 8
    pa = x + core * (y - x)
    pb = y + core * (x - y)
    other = 1 - core
    ap, am, a2 = (pa + 1) % 4, (pa + 3) % 4, (pa + 2) % 4
    bp, bm, b2 = (pb + 1) % 4, (pb + 3) % 4, (pb + 2) % 4
    sib = {"label": me + 1 - 2 * core}
    to_ap = {"label": lid(ap, pb, core)}
    to_am = {"label": lid(am, pb, core)}
    to_a2 = {"label": lid(a2, pb, core)}
    to_bp = {"label": lid(pa, bp, core)}
    to_bm = {"label": lid(pa, bm, core)}
    to_b2 = {"label": lid(pa, b2, core)}
    to_z = [None] + [{"dp": (z + dz) % NZ} for dz in range(1, NZ)]

    barrier = pltpu.get_barrier_semaphore()
    greeted = [sib, to_ap, to_am, to_a2, to_bp, to_bm, to_b2] + to_z[1:]
    for device in greeted:
        pl.semaphore_signal(barrier, inc=1, device_id=device, device_id_type=MESH)

    loads = []
    for j in range(D // LB):
        loads.append(pltpu.make_async_copy(
            head_in.at[:, pl.ds(j * LB, LB)], wl.at[me, pl.ds(j * LB, LB)], ls.at[j]))
    loads.append(pltpu.make_async_copy(proj_in, proj, ls.at[6]))
    loads.append(pltpu.make_async_copy(enc_in, enc, ls.at[7]))
    small = [
        pltpu.make_async_copy(num_in, num, ls.at[8]),
        pltpu.make_async_copy(den_in, den, ls.at[9]),
    ]
    loads.append(pltpu.make_async_copy(post_in, post, ls.at[10]))
    for load in small + loads:
        load.start()
    for load in small:
        load.wait()
    line = lax.broadcasted_iota(jnp.int32, (16, LB), 0)
    tail = jnp.where(line == 0, num[...], jnp.where(line == 1, den[...], 1))
    wl[me, D:SHARD, :] = tail.astype(F32).astype(BF16)

    count = [0]
    sent = []

    def take(n=1):
        first = count[0]
        count[0] += n
        return first

    def remote(src, dst, i, device):
        return pltpu.make_async_remote_copy(
            src_ref=src, dst_ref=dst, send_sem=ss.at[i], recv_sem=rs.at[i],
            device_id=device, device_id_type=MESH,
        )

    def send(src, dst, i, device):
        copy = remote(src, dst, i, device)
        copy.start()
        sent.append(copy)

    def landed(dst, i):
        remote(dst, dst, i, sib).wait_recv()

    def hidden_chunk(i):
        for b in (2 * i, 2 * i + 1):
            pos[b] = post[:, b * SB:(b + 1) * SB].T
        rows = enc[pl.ds(256 * i, 256), :]
        value = jnp.dot(rows, proj[...], preferred_element_type=F32).astype(BF16)
        hid[2 * i] = value[:SB]
        hid[2 * i + 1] = value[SB:]
        hidt[2 * i] = value[:SB].T
        hidt[2 * i + 1] = value[SB:].T
        enct[i] = rows.T

    share = take(8)

    def share_chunk(i):
        pair = pl.ds(2 * i, 2)
        send(hidt.at[pair], hidt_s.at[pair], share + 2 * i, sib)
        send(enct.at[i], enct_s.at[i], share + 2 * i + 1, sib)

    for load in loads[:6]:
        load.wait()
    pl.semaphore_wait(barrier, len(greeted))
    top, bottom = pl.ds(0, HALF0), pl.ds(HALF0, HALF1)
    first = take(3)
    base = take(16)
    near = take(16)

    def slot(a, b):
        return wl.at[lid(a, b, core)]

    columns = [pa, am, ap, a2]
    own = wl.at[me]
    early = [remote(own, own, first, to_ap), remote(own, own, first + 1, to_am)]
    for copy in early:
        copy.start()
    send(own, own, first + 2, to_a2)
    send(own, own, near, sib)
    for copy in early:
        copy.wait_send()
    send(own, own, base, to_bp)
    send(own, own, base + 1, to_bm)
    tabled = take()
    send(tab, tab_s, tabled, sib)
    loads[6].wait()
    loads[7].wait()
    loads[8].wait()
    hidden_chunk(0)

    def spread(j):
        held = slot(columns[j], pb)
        send(held, held, base + 4 * j, to_bp)
        send(held, held, base + 4 * j + 1, to_bm)
        send(held, held, near + j, sib)

    def forward(j):
        a = columns[j]
        held = slot(a, bm)
        landed(held, base + 4 * j)
        send(held.at[top], held.at[top], base + 4 * j + 2, to_bp)
        send(held, held, near + 4 + j, sib)
        held = slot(a, bp)
        landed(held, base + 4 * j + 1)
        send(held.at[bottom], held.at[bottom], base + 4 * j + 3, to_bm)
        send(held, held, near + 8 + j, sib)

    landed(slot(am, pb), first)
    spread(1)
    landed(slot(ap, pb), first + 1)
    spread(2)
    forward(0)
    landed(slot(a2, pb), first + 2)
    spread(3)
    share_chunk(0)
    hidden_chunk(1)
    forward(1)
    share_chunk(1)
    hidden_chunk(2)
    forward(2)
    share_chunk(2)
    hidden_chunk(3)
    forward(3)
    share_chunk(3)
    for j in (0, 1, 2, 3):
        held = slot(columns[j], b2)
        landed(held.at[top], base + 4 * j + 2)
        landed(held.at[bottom], base + 4 * j + 3)
        send(held, held, near + 12 + j, sib)
    for i in range(16):
        landed(own, near + i)

    place = lax.broadcasted_iota(jnp.int32, (SB, LB), 1)

    lent = take(16)

    def lend_gl(b):
        rows = pl.ds(pl.multiple_of(b * BEAM, BEAM), BEAM)
        return remote(gl.at[rows], gl_s.at[rows], lent + b, sib)

    def lend_gh(b):
        rows = pl.ds(pl.multiple_of(b * SB, SB), SB)
        return remote(gh.at[rows], gh_s.at[rows], lent + 8 + b, sib)

    def block(b, carry):
        wanted = pos[b]
        for k in range(BEAM):
            c = sl[k, b]
            for j in range(D // LB):
                w4[k * LB:(k + 1) * LB, j * LB:(j + 1) * LB] = wl[c, j * LB:(j + 1) * LB, :]
        rows = hid[b]
        parts = []
        for k in range(BEAM):
            c = sl[k, b]
            ends = wl[c, D:SHARD, :].astype(F32)
            scale = ends[0:1] / ends[1:2]
            logits = lax.dot_general(
                rows, w4[k * LB:(k + 1) * LB, :], (((1,), (1,)), ((), ())),
                preferred_element_type=F32,
            )
            hit = wanted[:, 0:1] == place + k * LB
            for column in range(1, wanted.shape[1]):
                hit = hit | (wanted[:, column:column + 1] == place + k * LB)
            target = jnp.where(hit, 1.0, 0.0)
            part = (scale * (jax.nn.sigmoid(logits) - target) / SB).astype(BF16)
            gl[b * BEAM + k] = part
            parts.append(part)

        @pl.when(b > 0)
        def _():
            lend_gl(b - 1).start()
            lend_gh(b - 1).start()

        total = jnp.dot(jnp.concatenate(parts, axis=1), w4[...], preferred_element_type=F32)
        gh[pl.ds(pl.multiple_of(b * SB, SB), SB), :] = total.astype(BF16)
        return carry

    lax.fori_loop(0, NBLK, block, 0)

    lend_gl(NBLK - 1).start()

    def proj_part(left, right, j, n):
        lanes = pl.ds(pl.multiple_of(core * (D // 2) + j * LB, 128), n * LB)
        whole = jnp.concatenate([left[i] for i in range(4)], axis=1)
        return jnp.dot(whole, right[:, lanes], preferred_element_type=F32)

    value = proj_part(enct, gh, 0, 1)
    lend_gh(NBLK - 1).start()
    pf[0:D, :] = value
    value = proj_part(enct, gh, 1, 2)
    pf[D:2 * D, :] = value[:, :LB]
    pf[2 * D:3 * D, :] = value[:, LB:]
    for i in range(4):
        landed(enct_s.at[i], share + 2 * i + 1)

    def arrive_gh(b, carry):
        lend_gh(b).wait_recv()
        return carry

    lax.fori_loop(0, NBLK, arrive_gh, 0)
    value = proj_part(enct_s, gh_s, 0, 3)
    for j in range(3):
        rows = slice(j * D, (j + 1) * D)
        pf[rows, :] = pf[rows, :] + value[:, j * LB:(j + 1) * LB]

    def ablk(a):
        return pl.ds(pl.multiple_of(a * ABLK, 16), ABLK)

    pm = take(3)
    mine = ablk(pa)
    pas[2] = pf[ablk(a2), :].astype(BF16)
    pas[0] = pf[ablk(ap), :].astype(BF16)
    pas[1] = pf[ablk(am), :].astype(BF16)
    for i in range(4):
        landed(hidt_s.at[pl.ds(2 * i, 2)], share + 2 * i)
    landed(tab_s, tabled)

    def arrive_gl(b, carry):
        lend_gl(b).wait_recv()
        return carry

    lax.fori_loop(0, NBLK, arrive_gl, 0)
    send(pas.at[2], pra.at[2], pm + 2, to_a2)
    send(pas.at[0], pra.at[0], pm, to_ap)
    send(pas.at[1], pra.at[1], pm + 1, to_am)

    hm = take(12)

    def along_a(db, r):
        return remote(cb.at[db * 3 + r], ra.at[r, db], hm + db * 3 + r, (to_ap, to_am, to_a2)[r])

    def halves(c, table, turned, grads):
        code = table[0, c]
        one = lax.rem(code, 32)
        two = lax.rem(lax.div(code, 32), 32)
        total = lax.div(code, 1024)
        up = grads[one].astype(F32) * jnp.minimum(total, 1).astype(F32)
        down = grads[two].astype(F32) * jnp.maximum(total - 1, 0).astype(F32)
        left = [turned[lax.div(one, BEAM)], turned[lax.div(two, BEAM)]]
        return left, [up.astype(BF16), down.astype(BF16)]

    def own_clusters(db, carry):
        def value_of(da):
            c = lid((pa + 6 - da) % 4, (pb + 6 - db) % 4, core)
            left, right = halves(c, tab, hidt, gl)
            left_s, right_s = halves(c, tab_s, hidt_s, gl_s)
            return jnp.dot(
                jnp.concatenate(left + left_s, axis=1),
                jnp.concatenate(right + right_s, axis=0),
                preferred_element_type=F32,
            )

        cb[db * 3 + 2] = value_of(0).astype(BF16)
        cb[db * 3] = value_of(1).astype(BF16)
        along_a(db, 2).start()
        cb[db * 3 + 1] = value_of(3).astype(BF16)
        along_a(db, 0).start()
        cf[db] = value_of(2)
        along_a(db, 1).start()
        return carry

    lax.fori_loop(0, 2, own_clusters, 0)
    lax.fori_loop(3, 4, own_clusters, 0)

    outs = []

    def enc_chunk(i):
        rows = pl.ds(256 * i, 256)
        ge[rows, :] = lax.dot_general(
            gh[rows, :], proj[...], (((1,), (1,)), ((), ())), preferred_element_type=F32
        )

    for r in range(3):
        landed(pra.at[r], pm + r)
    value = pf[mine, :] + pra[0].astype(F32) + pra[1].astype(F32) + pra[2].astype(F32)
    pf[mine, :] = value
    pbs[...] = value.astype(BF16)

    def piece(b):
        return pl.ds(pl.multiple_of(b * PIECE, 16), PIECE)

    pn = take(3)
    lax.fori_loop(2, 3, own_clusters, 0)
    send(pbs.at[piece(b2)], prb.at[2], pn + 2, to_b2)
    send(pbs.at[piece(bp)], prb.at[0], pn, to_bp)
    send(pbs.at[piece(bm)], prb.at[1], pn + 1, to_bm)
    hn = take(3)
    enc_chunk(0)
    enc_chunk(1)

    def finish_a(db):
        for r in range(3):
            landed(ra.at[r, db], hm + db * 3 + r)
        return cf[db] + ra[0, db].astype(F32) + ra[1, db].astype(F32) + ra[2, db].astype(F32)

    for r in range(3):
        landed(prb.at[r], pn + r)
    spot_rows = pl.ds(pl.multiple_of(pa * ABLK + pb * PIECE, 16), PIECE)
    value = pf[spot_rows, :] + prb[0].astype(F32) + prb[1].astype(F32) + prb[2].astype(F32)
    ez[...] = value.astype(BF16)
    zp[z] = value.astype(BF16)
    pz = take(NZ)
    dbs[2] = finish_a(0).astype(BF16)
    for dz in (4, 3, 5, 2, 6, 1, 7):
        send(ez, zp.at[z], pz + dz, to_z[dz])
    enc_chunk(2)
    send(dbs.at[2], rbb.at[2], hn + 2, to_b2)
    dbs[0] = finish_a(1).astype(BF16)
    enc_chunk(3)
    send(dbs.at[0], rbb.at[0], hn, to_bp)
    dbs[1] = finish_a(3).astype(BF16)
    for dz in range(1, NZ):
        landed(zp.at[(z + NZ - dz) % NZ], pz + dz)
    send(dbs.at[1], rbb.at[1], hn + 1, to_bm)
    total = zp[0].astype(F32)
    for i in range(1, NZ):
        total = total + zp[i].astype(F32)

    def spot(a, b):
        return po.at[pl.ds(pl.multiple_of((core * 4 + a) * ABLK + b * PIECE, 16), PIECE)]

    po[pl.ds(pl.multiple_of((core * 4 + pa) * ABLK + pb * PIECE, 16), PIECE), :] = total.astype(BF16)
    g1 = take(3)
    g2 = take(12)
    g3 = take(16)
    along = [pb, bm, bp, b2]
    hops = [am, ap, a2]

    def outward(q):
        held = spot(pa, along[q])
        for r, device in enumerate((to_ap, to_am, to_a2)):
            send(held, held, g2 + 3 * q + r, device)
        send(held, held, g3 + q, sib)

    held = spot(pa, pb)
    for r, device in enumerate((to_bp, to_bm, to_b2)):
        send(held, held, g1 + r, device)
    outward(0)
    value = finish_a(2)
    for r in (2, 0, 1):
        landed(rbb.at[r], hn + r)
    value = value + rbb[0].astype(F32) + rbb[1].astype(F32) + rbb[2].astype(F32)
    value = value.reshape(NZ, D // NZ, LB)
    ef[...] = value
    zs[...] = value.astype(BF16)
    hz = take(NZ)
    for q in (1, 2, 3):
        landed(spot(pa, along[q]), g1 + q - 1)
        outward(q)
    for dz in (4, 3, 5, 2, 6, 1, 7):
        send(zs.at[(z + dz) % NZ], zr.at[dz], hz + dz, to_z[dz])
    for q in range(4):
        for r in range(3):
            held = spot(hops[r], along[q])
            landed(held, g2 + 3 * q + r)
            send(held, held, g3 + 4 + 3 * q + r, sib)
    for dz in range(1, NZ):
        landed(zr.at[dz], hz + dz)
    value = ef[z]
    for dz in range(1, NZ):
        value = value + zr[dz].astype(F32)
    gh_out[...] = value
    for i in range(16):
        landed(spot(pa, pb), g3 + i)
    for j in range(D // LB):
        copy = pltpu.make_async_copy(
            po.at[pl.ds(j * D, D)], gp_out.at[:, pl.ds(j * LB, LB)], ls.at[j])
        copy.start()
        outs.append(copy)
    for copy in sent:
        copy.wait_send()

    def drain(i, carry):
        lend_gl(i).wait_send()
        lend_gh(i).wait_send()
        return carry

    lax.fori_loop(0, NBLK, drain, 0)

    def drain_a(db, carry):
        for r in range(3):
            along_a(db, r).wait_send()
        return carry

    lax.fori_loop(0, 4, drain_a, 0)
    for copy in outs:
        copy.wait()
    assert count[0] <= MESSAGES, count[0]


MESSAGES = 160


def scratch():
    v = pltpu.VMEM
    return [
        v((1, LB), jnp.int32), v((1, LB), jnp.int32), v((8, ROWS), jnp.int32),
        v((ROWS, D), BF16), v((D, D), BF16),
        v((32, SHARD, LB), BF16), v((NBLK, SB, 8), jnp.int32),
        v((NBLK, SB, D), BF16), v((NBLK, D, SB), BF16), v((NBLK, D, SB), BF16),
        v((4, D, ROWS // 4), BF16), v((4, D, ROWS // 4), BF16),
        v((BEAM * LB, D), BF16), v((32, SB, LB), BF16), v((32, SB, LB), BF16),
        v((ROWS, D), BF16), v((ROWS, D), BF16),
        v((12, D, LB), BF16), v((4, D, LB), F32),
        v((3, 4, D, LB), BF16), v((3, D, LB), BF16), v((3, D, LB), BF16),
        v((NZ, D // NZ, LB), F32), v((NZ, D // NZ, LB), BF16), v((NZ, D // NZ, LB), BF16),
        v((CORE, LB), F32),
        v((3, ABLK, LB), BF16), v((3, ABLK, LB), BF16),
        v((ABLK, LB), BF16), v((3, PIECE, LB), BF16),
        v((PIECE, LB), BF16), v((NZ, PIECE, LB), BF16), v((2 * CORE, LB), BF16),
        pltpu.SMEM((1, 128), jnp.int32),
        pltpu.SemaphoreType.DMA((MESSAGES,)), pltpu.SemaphoreType.DMA((MESSAGES,)),
        pltpu.SemaphoreType.DMA((12,)),
    ]


def shards(enc, proj, head_weight, shortlist, positives, weight_num, weight_den):
    ids = jnp.arange(32, dtype=jnp.int32)[:, None, None]
    match = shortlist[None] == ids
    order = jnp.arange(NBLK * BEAM, dtype=jnp.int32).reshape(1, NBLK, BEAM)
    total = jnp.sum(match.astype(jnp.int32), axis=(1, 2))
    one = jnp.min(jnp.where(match, order, NBLK * BEAM - 1), axis=(1, 2))
    two = jnp.max(jnp.where(match, order, 0), axis=(1, 2))
    tab = jnp.pad(one + 32 * two + 1024 * total, (0, 96)).reshape(1, 128)
    smem = pl.BlockSpec(memory_space=pltpu.SMEM)
    vmem = pl.BlockSpec(memory_space=pltpu.VMEM)
    anyspace = pl.BlockSpec(memory_space=pl.ANY)
    grad_enc, grad_proj, grad_head = pl.pallas_call(
        kernel,
        out_shape=(
            pltpu.VMEM((ROWS, D), F32),
            jax.ShapeDtypeStruct((D, D), BF16),
            jax.ShapeDtypeStruct((D // NZ, LB), F32),
        ),
        in_specs=[smem, smem] + [pl.BlockSpec(memory_space=pltpu.HBM)] * 6,
        out_specs=(vmem, anyspace, vmem),
        scratch_shapes=scratch(),
        compiler_params=pltpu.CompilerParams(
            collective_id=0, has_side_effects=True, vmem_limit_bytes=56 << 20
        ),
    )(
        shortlist.T, tab, weight_num.reshape(1, LB), weight_den.reshape(1, LB), positives.T,
        enc, proj, head_weight,
    )
    return (grad_enc, grad_proj.astype(F32), grad_head.T)


def solution(mesh):
    placed = (
        P(("dp", "label"), None),
        P(),
        P("label", None),
        P(("dp", "label"), None),
        P(("dp", "label"), None),
        P("label"),
        P("label"),
    )
    return jax.shard_map(
        shards,
        mesh=mesh,
        in_specs=placed,
        out_specs=(P(("dp", "label"), None), P(), P("label", "dp")),
        check_vma=False,
    )
```

```python
import jax
import jax.numpy as jnp
from jax import lax
from jax.experimental import pallas as pl
from jax.experimental.pallas import tpu as pltpu
from jax.sharding import PartitionSpec as P

MESH = pl.DeviceIdType.MESH
F32 = jnp.float32
BF16 = jnp.bfloat16

D = 768
LB = 128
SB = 128
BEAM = 4
NBLK = 8
ROWS = NBLK * SB
SHARD = D + 16
HALF0, HALF1 = 400, 384
NZ = 8
PIECE = 144
ABLK = 4 * PIECE
CORE = 4 * ABLK


def lid(pa, pb, core):
    xx = pa + core * (pb - pa)
    yy = pb + core * (pa - pb)
    return (yy * 4 + xx) * 2 + core


def kernel(
    sl, num_in, den_in, post_in, enc_in, proj_in, head_in,
    ge, gp_out, gh_out,
    num, den, post, enc, proj, wl, pos, hid, hidt, hidt_s, enct, enct_s, w4, gl, gl_s, gh, gh_s,
    cb, cf, ra, dbs, rbb, ef, zs, zr,
    pf, pas, pra, pbs, prb, ez, zp, po, tab, tab_s,
    ss, rs, ls,
):
    z = lax.axis_index("dp")
    me = lax.axis_index("label")
    core = me % 2
    x = (me // 2) % 4
    y = me // 8
    pa = x + core * (y - x)
    pb = y + core * (x - y)
    other = 1 - core
    ap, am, a2 = (pa + 1) % 4, (pa + 3) % 4, (pa + 2) % 4
    bp, bm, b2 = (pb + 1) % 4, (pb + 3) % 4, (pb + 2) % 4
    sib = {"label": me + 1 - 2 * core}
    to_ap = {"label": lid(ap, pb, core)}
    to_am = {"label": lid(am, pb, core)}
    to_a2 = {"label": lid(a2, pb, core)}
    to_bp = {"label": lid(pa, bp, core)}
    to_bm = {"label": lid(pa, bm, core)}
    to_b2 = {"label": lid(pa, b2, core)}
    to_z = [None] + [{"dp": (z + dz) % NZ} for dz in range(1, NZ)]

    barrier = pltpu.get_barrier_semaphore()
    greeted = [sib, to_ap, to_am, to_a2, to_bp, to_bm, to_b2] + to_z[1:]
    for device in greeted:
        pl.semaphore_signal(barrier, inc=1, device_id=device, device_id_type=MESH)

    loads = []
    for j in range(D // LB):
        loads.append(pltpu.make_async_copy(
            head_in.at[:, pl.ds(j * LB, LB)], wl.at[me, pl.ds(j * LB, LB)], ls.at[j]))
    loads.append(pltpu.make_async_copy(proj_in, proj, ls.at[6]))
    loads.append(pltpu.make_async_copy(enc_in, enc, ls.at[7]))
    small = [
        pltpu.make_async_copy(num_in, num, ls.at[8]),
        pltpu.make_async_copy(den_in, den, ls.at[9]),
    ]
    loads.append(pltpu.make_async_copy(post_in, post, ls.at[10]))
    for load in small + loads:
        load.start()
    for load in small:
        load.wait()
    line = lax.broadcasted_iota(jnp.int32, (16, LB), 0)
    tail = jnp.where(line == 0, num[...], jnp.where(line == 1, den[...], 1))
    wl[me, D:SHARD, :] = tail.astype(F32).astype(BF16)

    count = [0]
    sent = []

    def take(n=1):
        first = count[0]
        count[0] += n
        return first

    def remote(src, dst, i, device):
        return pltpu.make_async_remote_copy(
            src_ref=src, dst_ref=dst, send_sem=ss.at[i], recv_sem=rs.at[i],
            device_id=device, device_id_type=MESH,
        )

    def send(src, dst, i, device):
        copy = remote(src, dst, i, device)
        copy.start()
        sent.append(copy)

    def landed(dst, i):
        remote(dst, dst, i, sib).wait_recv()

    def hidden_chunk(i):
        for b in (2 * i, 2 * i + 1):
            pos[b] = post[:, b * SB:(b + 1) * SB].T
        rows = enc[pl.ds(256 * i, 256), :]
        value = jnp.dot(rows, proj[...], preferred_element_type=F32).astype(BF16)
        hid[2 * i] = value[:SB]
        hid[2 * i + 1] = value[SB:]
        hidt[2 * i] = value[:SB].T
        hidt[2 * i + 1] = value[SB:].T
        enct[i] = rows.T

    share = take(8)

    def share_chunk(i):
        pair = pl.ds(2 * i, 2)
        send(hidt.at[pair], hidt_s.at[pair], share + 2 * i, sib)
        send(enct.at[i], enct_s.at[i], share + 2 * i + 1, sib)

    def name_pairs(c, carry):
        one, two, total = jnp.int32(0), jnp.int32(0), jnp.int32(0)
        for p in range(NBLK * BEAM):
            two = jnp.where(sl[p % BEAM, p // BEAM] == c, p, two)
            total = total + jnp.where(sl[p % BEAM, p // BEAM] == c, 1, 0)
        for p in reversed(range(NBLK * BEAM)):
            one = jnp.where(sl[p % BEAM, p // BEAM] == c, p, one)
        tab[0, c] = one + 32 * two + 1024 * total
        return carry


    for load in loads[:6]:
        load.wait()
    pl.semaphore_wait(barrier, len(greeted))
    top, bottom = pl.ds(0, HALF0), pl.ds(HALF0, HALF1)
    first = take(3)
    base = take(16)
    near = take(16)

    def slot(a, b):
        return wl.at[lid(a, b, core)]

    columns = [pa, am, ap, a2]
    own = wl.at[me]
    early = [remote(own, own, first, to_ap), remote(own, own, first + 1, to_am)]
    for copy in early:
        copy.start()
    send(own, own, first + 2, to_a2)
    send(own, own, near, sib)
    for copy in early:
        copy.wait_send()
    send(own, own, base, to_bp)
    send(own, own, base + 1, to_bm)
    loads[6].wait()
    loads[7].wait()
    loads[8].wait()
    hidden_chunk(0)

    def spread(j):
        held = slot(columns[j], pb)
        send(held, held, base + 4 * j, to_bp)
        send(held, held, base + 4 * j + 1, to_bm)
        send(held, held, near + j, sib)

    def forward(j):
        a = columns[j]
        held = slot(a, bm)
        landed(held, base + 4 * j)
        send(held.at[top], held.at[top], base + 4 * j + 2, to_bp)
        send(held, held, near + 4 + j, sib)
        held = slot(a, bp)
        landed(held, base + 4 * j + 1)
        send(held.at[bottom], held.at[bottom], base + 4 * j + 3, to_bm)
        send(held, held, near + 8 + j, sib)

    landed(slot(am, pb), first)
    spread(1)
    landed(slot(ap, pb), first + 1)
    spread(2)
    forward(0)
    landed(slot(a2, pb), first + 2)
    spread(3)
    share_chunk(0)
    hidden_chunk(1)
    forward(1)
    share_chunk(1)
    hidden_chunk(2)
    forward(2)
    share_chunk(2)
    hidden_chunk(3)
    forward(3)
    share_chunk(3)
    for j in (0, 1, 2, 3):
        held = slot(columns[j], b2)
        landed(held.at[top], base + 4 * j + 2)
        landed(held.at[bottom], base + 4 * j + 3)
        send(held, held, near + 12 + j, sib)
        if j == 1:
            lax.fori_loop(0, 32, name_pairs, 0)
            for c in range(32, LB):
                tab[0, c] = 0
    for i in range(16):
        landed(own, near + i)

    tabled = take()
    send(tab, tab_s, tabled, sib)

    place = lax.broadcasted_iota(jnp.int32, (SB, LB), 1)

    lent = take(16)

    def lend_gl(b):
        rows = pl.ds(pl.multiple_of(b * BEAM, BEAM), BEAM)
        return remote(gl.at[rows], gl_s.at[rows], lent + b, sib)

    def lend_gh(b):
        rows = pl.ds(pl.multiple_of(b * SB, SB), SB)
        return remote(gh.at[rows], gh_s.at[rows], lent + 8 + b, sib)

    def block(b, carry):
        wanted = pos[b]
        for k in range(BEAM):
            c = sl[k, b]
            for j in range(D // LB):
                w4[k * LB:(k + 1) * LB, j * LB:(j + 1) * LB] = wl[c, j * LB:(j + 1) * LB, :]
        rows = hid[b]
        parts = []
        for k in range(BEAM):
            c = sl[k, b]
            ends = wl[c, D:SHARD, :].astype(F32)
            scale = ends[0:1] / ends[1:2]
            logits = lax.dot_general(
                rows, w4[k * LB:(k + 1) * LB, :], (((1,), (1,)), ((), ())),
                preferred_element_type=F32,
            )
            hit = wanted[:, 0:1] == place + k * LB
            for column in range(1, wanted.shape[1]):
                hit = hit | (wanted[:, column:column + 1] == place + k * LB)
            target = jnp.where(hit, 1.0, 0.0)
            part = (scale * (jax.nn.sigmoid(logits) - target) / SB).astype(BF16)
            gl[b * BEAM + k] = part
            parts.append(part)

        @pl.when(b > 0)
        def _():
            lend_gl(b - 1).start()
            lend_gh(b - 1).start()

        total = jnp.dot(jnp.concatenate(parts, axis=1), w4[...], preferred_element_type=F32)
        gh[pl.ds(pl.multiple_of(b * SB, SB), SB), :] = total.astype(BF16)
        return carry

    lax.fori_loop(0, NBLK, block, 0)

    lend_gl(NBLK - 1).start()

    def proj_part(left, right, j, n):
        lanes = pl.ds(pl.multiple_of(core * (D // 2) + j * LB, 128), n * LB)
        whole = jnp.concatenate([left[i] for i in range(4)], axis=1)
        return jnp.dot(whole, right[:, lanes], preferred_element_type=F32)

    value = proj_part(enct, gh, 0, 1)
    lend_gh(NBLK - 1).start()
    pf[0:D, :] = value
    value = proj_part(enct, gh, 1, 2)
    pf[D:2 * D, :] = value[:, :LB]
    pf[2 * D:3 * D, :] = value[:, LB:]
    for i in range(4):
        landed(enct_s.at[i], share + 2 * i + 1)

    def arrive_gh(b, carry):
        lend_gh(b).wait_recv()
        return carry

    lax.fori_loop(0, NBLK, arrive_gh, 0)
    value = proj_part(enct_s, gh_s, 0, 3)
    for j in range(3):
        rows = slice(j * D, (j + 1) * D)
        pf[rows, :] = pf[rows, :] + value[:, j * LB:(j + 1) * LB]

    def ablk(a):
        return pl.ds(pl.multiple_of(a * ABLK, 16), ABLK)

    pm = take(3)
    mine = ablk(pa)
    pas[2] = pf[ablk(a2), :].astype(BF16)
    pas[0] = pf[ablk(ap), :].astype(BF16)
    pas[1] = pf[ablk(am), :].astype(BF16)
    for i in range(4):
        landed(hidt_s.at[pl.ds(2 * i, 2)], share + 2 * i)
    landed(tab_s, tabled)

    def arrive_gl(b, carry):
        lend_gl(b).wait_recv()
        return carry

    lax.fori_loop(0, NBLK, arrive_gl, 0)
    send(pas.at[2], pra.at[2], pm + 2, to_a2)
    send(pas.at[0], pra.at[0], pm, to_ap)
    send(pas.at[1], pra.at[1], pm + 1, to_am)

    hm = take(12)

    def along_a(db, r):
        return remote(cb.at[db * 3 + r], ra.at[r, db], hm + db * 3 + r, (to_ap, to_am, to_a2)[r])

    def halves(c, table, turned, grads):
        code = table[0, c]
        one = lax.rem(code, 32)
        two = lax.rem(lax.div(code, 32), 32)
        total = lax.div(code, 1024)
        up = grads[one].astype(F32) * jnp.minimum(total, 1).astype(F32)
        down = grads[two].astype(F32) * jnp.maximum(total - 1, 0).astype(F32)
        left = [turned[lax.div(one, BEAM)], turned[lax.div(two, BEAM)]]
        return left, [up.astype(BF16), down.astype(BF16)]

    def own_clusters(db, carry):
        def value_of(da):
            c = lid((pa + 6 - da) % 4, (pb + 6 - db) % 4, core)
            left, right = halves(c, tab, hidt, gl)
            left_s, right_s = halves(c, tab_s, hidt_s, gl_s)
            return jnp.dot(
                jnp.concatenate(left + left_s, axis=1),
                jnp.concatenate(right + right_s, axis=0),
                preferred_element_type=F32,
            )

        cb[db * 3 + 2] = value_of(0).astype(BF16)
        cb[db * 3] = value_of(1).astype(BF16)
        along_a(db, 2).start()
        cb[db * 3 + 1] = value_of(3).astype(BF16)
        along_a(db, 0).start()
        cf[db] = value_of(2)
        along_a(db, 1).start()
        return carry

    lax.fori_loop(0, 2, own_clusters, 0)
    lax.fori_loop(3, 4, own_clusters, 0)

    def enc_chunk(i):
        rows = pl.ds(256 * i, 256)
        ge[rows, :] = lax.dot_general(
            gh[rows, :], proj[...], (((1,), (1,)), ((), ())), preferred_element_type=F32
        )

    for r in range(3):
        landed(pra.at[r], pm + r)
    value = pf[mine, :] + pra[0].astype(F32) + pra[1].astype(F32) + pra[2].astype(F32)
    pf[mine, :] = value
    pbs[...] = value.astype(BF16)

    def piece(b):
        return pl.ds(pl.multiple_of(b * PIECE, 16), PIECE)

    pn = take(3)
    lax.fori_loop(2, 3, own_clusters, 0)
    send(pbs.at[piece(b2)], prb.at[2], pn + 2, to_b2)
    send(pbs.at[piece(bp)], prb.at[0], pn, to_bp)
    send(pbs.at[piece(bm)], prb.at[1], pn + 1, to_bm)
    hn = take(3)
    enc_chunk(0)
    enc_chunk(1)

    def finish_a(db):
        for r in range(3):
            landed(ra.at[r, db], hm + db * 3 + r)
        return cf[db] + ra[0, db].astype(F32) + ra[1, db].astype(F32) + ra[2, db].astype(F32)

    for r in range(3):
        landed(prb.at[r], pn + r)
    spot_rows = pl.ds(pl.multiple_of(pa * ABLK + pb * PIECE, 16), PIECE)
    value = pf[spot_rows, :] + prb[0].astype(F32) + prb[1].astype(F32) + prb[2].astype(F32)
    ez[...] = value.astype(BF16)
    zp[z] = value.astype(BF16)
    pz = take(NZ)
    dbs[2] = finish_a(0).astype(BF16)
    for dz in (4, 3, 5, 2, 6, 1, 7):
        send(ez, zp.at[z], pz + dz, to_z[dz])
    enc_chunk(2)
    send(dbs.at[2], rbb.at[2], hn + 2, to_b2)
    dbs[0] = finish_a(1).astype(BF16)
    enc_chunk(3)
    send(dbs.at[0], rbb.at[0], hn, to_bp)
    dbs[1] = finish_a(3).astype(BF16)
    for dz in range(1, NZ):
        landed(zp.at[(z + NZ - dz) % NZ], pz + dz)
    send(dbs.at[1], rbb.at[1], hn + 1, to_bm)
    total = zp[0].astype(F32)
    for i in range(1, NZ):
        total = total + zp[i].astype(F32)

    def spot(a, b):
        return po.at[pl.ds(pl.multiple_of((core * 4 + a) * ABLK + b * PIECE, 16), PIECE)]

    po[pl.ds(pl.multiple_of((core * 4 + pa) * ABLK + pb * PIECE, 16), PIECE), :] = total.astype(BF16)
    g1 = take(3)
    g2 = take(12)
    g3 = take(16)
    along = [pb, bm, bp, b2]
    hops = [am, ap, a2]

    def outward(q):
        held = spot(pa, along[q])
        for r, device in enumerate((to_ap, to_am, to_a2)):
            send(held, held, g2 + 3 * q + r, device)
        send(held, held, g3 + q, sib)

    held = spot(pa, pb)
    for r, device in enumerate((to_bp, to_bm, to_b2)):
        send(held, held, g1 + r, device)
    outward(0)
    value = finish_a(2)
    for r in (2, 0, 1):
        landed(rbb.at[r], hn + r)
    value = value + rbb[0].astype(F32) + rbb[1].astype(F32) + rbb[2].astype(F32)
    value = value.reshape(NZ, D // NZ, LB)
    zs[...] = value.astype(BF16)
    ef[...] = value
    hz = take(NZ)
    for dz in (4, 3, 5, 2, 6, 1, 7):
        send(zs.at[(z + dz) % NZ], zr.at[dz], hz + dz, to_z[dz])
    for q in (1, 2, 3):
        landed(spot(pa, along[q]), g1 + q - 1)
        outward(q)
    for q in range(4):
        for r in range(3):
            held = spot(hops[r], along[q])
            landed(held, g2 + 3 * q + r)
            send(held, held, g3 + 4 + 3 * q + r, sib)
    for dz in range(1, NZ):
        landed(zr.at[dz], hz + dz)
    value = ef[z]
    for dz in range(1, NZ):
        value = value + zr[dz].astype(F32)
    gh_out[...] = value

    def widen(which):
        for j in range(3):
            lanes = pl.ds(pl.multiple_of((which * 3 + j) * LB, LB), LB)
            rows = pl.ds(pl.multiple_of(which * CORE + j * D, 16), D)
            gp_out[:, lanes] = po[rows, :].astype(F32)

    widen(core)
    for i in range(16):
        landed(spot(pa, pb), g3 + i)
    widen(other)
    for copy in sent:
        copy.wait_send()

    def drain(i, carry):
        lend_gl(i).wait_send()
        lend_gh(i).wait_send()
        return carry

    lax.fori_loop(0, NBLK, drain, 0)

    def drain_a(db, carry):
        for r in range(3):
            along_a(db, r).wait_send()
        return carry

    lax.fori_loop(0, 4, drain_a, 0)
    assert count[0] <= MESSAGES, count[0]


MESSAGES = 160


def scratch():
    v = pltpu.VMEM
    return [
        v((1, LB), jnp.int32), v((1, LB), jnp.int32), v((8, ROWS), jnp.int32),
        v((ROWS, D), BF16), v((D, D), BF16),
        v((32, SHARD, LB), BF16), v((NBLK, SB, 8), jnp.int32),
        v((NBLK, SB, D), BF16), v((NBLK, D, SB), BF16), v((NBLK, D, SB), BF16),
        v((4, D, ROWS // 4), BF16), v((4, D, ROWS // 4), BF16),
        v((BEAM * LB, D), BF16), v((32, SB, LB), BF16), v((32, SB, LB), BF16),
        v((ROWS, D), BF16), v((ROWS, D), BF16),
        v((12, D, LB), BF16), v((4, D, LB), F32),
        v((3, 4, D, LB), BF16), v((3, D, LB), BF16), v((3, D, LB), BF16),
        v((NZ, D // NZ, LB), F32), v((NZ, D // NZ, LB), BF16), v((NZ, D // NZ, LB), BF16),
        v((CORE, LB), F32),
        v((3, ABLK, LB), BF16), v((3, ABLK, LB), BF16),
        v((ABLK, LB), BF16), v((3, PIECE, LB), BF16),
        v((PIECE, LB), BF16), v((NZ, PIECE, LB), BF16), v((2 * CORE, LB), BF16),
        pltpu.SMEM((1, 128), jnp.int32), pltpu.SMEM((1, 128), jnp.int32),
        pltpu.SemaphoreType.DMA((MESSAGES,)), pltpu.SemaphoreType.DMA((MESSAGES,)),
        pltpu.SemaphoreType.DMA((12,)),
    ]


def shards(enc, proj, head_weight, shortlist, positives, weight_num, weight_den):
    smem = pl.BlockSpec(memory_space=pltpu.SMEM)
    vmem = pl.BlockSpec(memory_space=pltpu.VMEM)
    grad_enc, grad_proj, grad_head = pl.pallas_call(
        kernel,
        out_shape=(
            pltpu.VMEM((ROWS, D), F32),
            pltpu.VMEM((D, D), F32),
            pltpu.VMEM((D // NZ, LB), F32),
        ),
        in_specs=[smem] + [pl.BlockSpec(memory_space=pltpu.HBM)] * 6,
        out_specs=(vmem, vmem, vmem),
        scratch_shapes=scratch(),
        compiler_params=pltpu.CompilerParams(
            collective_id=0, has_side_effects=True, vmem_limit_bytes=56 << 20
        ),
    )(
        shortlist.T, weight_num.reshape(1, LB), weight_den.reshape(1, LB), positives.T,
        enc, proj, head_weight,
    )
    return (grad_enc, grad_proj, grad_head.T)


def solution(mesh):
    placed = (
        P(("dp", "label"), None),
        P(),
        P("label", None),
        P(("dp", "label"), None),
        P(("dp", "label"), None),
        P("label"),
        P("label"),
    )
    return jax.shard_map(
        shards,
        mesh=mesh,
        in_specs=placed,
        out_specs=(P(("dp", "label"), None), P(), P("label", "dp")),
        check_vma=False,
    )
```

```python
import jax
import jax.numpy as jnp
from jax import lax
from jax.experimental import pallas as pl
from jax.experimental.pallas import tpu as pltpu
from jax.sharding import PartitionSpec as P

MESH = pl.DeviceIdType.MESH
F32 = jnp.float32
BF16 = jnp.bfloat16

D = 768
LB = 128
SB = 128
BEAM = 4
NBLK = 8
ROWS = NBLK * SB
SHARD = D + 16
HALF0, HALF1 = 400, 384
NZ = 8
PIECE = 144
ABLK = 4 * PIECE
CORE = 4 * ABLK


def lid(pa, pb, core):
    xx = pa + core * (pb - pa)
    yy = pb + core * (pa - pb)
    return (yy * 4 + xx) * 2 + core


def kernel(
    sl, num_in, den_in, post_in, enc_in, proj_in, head_in,
    ge, gp_out, gh_out,
    num, den, post, enc, proj, wl, pos, hid, hidt, hidt_s, enct, enct_s, w4, gl, gl_s, gh, gh_s,
    cb, cf, ra, dbs, rbb, ef, zs, zr,
    pf, pas, pra, pbs, prb, ez, zp, po, tab, tab_s,
    ss, rs, ls,
):
    z = lax.axis_index("dp")
    me = lax.axis_index("label")
    core = me % 2
    x = (me // 2) % 4
    y = me // 8
    pa = x + core * (y - x)
    pb = y + core * (x - y)
    other = 1 - core
    ap, am, a2 = (pa + 1) % 4, (pa + 3) % 4, (pa + 2) % 4
    bp, bm, b2 = (pb + 1) % 4, (pb + 3) % 4, (pb + 2) % 4
    sib = {"label": me + 1 - 2 * core}
    to_ap = {"label": lid(ap, pb, core)}
    to_am = {"label": lid(am, pb, core)}
    to_a2 = {"label": lid(a2, pb, core)}
    to_bp = {"label": lid(pa, bp, core)}
    to_bm = {"label": lid(pa, bm, core)}
    to_b2 = {"label": lid(pa, b2, core)}
    to_z = [None] + [{"dp": (z + dz) % NZ} for dz in range(1, NZ)]

    barrier = pltpu.get_barrier_semaphore()
    greeted = [sib, to_ap, to_am, to_a2, to_bp, to_bm, to_b2] + to_z[1:]
    for device in greeted:
        pl.semaphore_signal(barrier, inc=1, device_id=device, device_id_type=MESH)

    loads = []
    for j in range(D // LB):
        loads.append(pltpu.make_async_copy(
            head_in.at[:, pl.ds(j * LB, LB)], wl.at[me, pl.ds(j * LB, LB)], ls.at[j]))
    loads.append(pltpu.make_async_copy(proj_in, proj, ls.at[6]))
    loads.append(pltpu.make_async_copy(enc_in, enc, ls.at[7]))
    small = [
        pltpu.make_async_copy(num_in, num, ls.at[8]),
        pltpu.make_async_copy(den_in, den, ls.at[9]),
    ]
    loads.append(pltpu.make_async_copy(post_in, post, ls.at[10]))
    for load in small + loads:
        load.start()
    for load in small:
        load.wait()
    line = lax.broadcasted_iota(jnp.int32, (16, LB), 0)
    tail = jnp.where(line == 0, num[...], jnp.where(line == 1, den[...], 1))
    wl[me, D:SHARD, :] = tail.astype(F32).astype(BF16)

    count = [0]
    sent = []

    def take(n=1):
        first = count[0]
        count[0] += n
        return first

    def remote(src, dst, i, device):
        return pltpu.make_async_remote_copy(
            src_ref=src, dst_ref=dst, send_sem=ss.at[i], recv_sem=rs.at[i],
            device_id=device, device_id_type=MESH,
        )

    def send(src, dst, i, device):
        copy = remote(src, dst, i, device)
        copy.start()
        sent.append(copy)

    def landed(dst, i):
        remote(dst, dst, i, sib).wait_recv()

    def hidden_chunk(i):
        for b in (2 * i, 2 * i + 1):
            pos[b] = post[:, b * SB:(b + 1) * SB].T
        rows = enc[pl.ds(256 * i, 256), :]
        value = jnp.dot(rows, proj[...], preferred_element_type=F32).astype(BF16)
        hid[2 * i] = value[:SB]
        hid[2 * i + 1] = value[SB:]
        hidt[2 * i] = value[:SB].T
        hidt[2 * i + 1] = value[SB:].T
        enct[i] = rows.T

    share = take(8)

    def share_chunk(i):
        pair = pl.ds(2 * i, 2)
        send(hidt.at[pair], hidt_s.at[pair], share + 2 * i, sib)
        send(enct.at[i], enct_s.at[i], share + 2 * i + 1, sib)

    def name_pairs(c, carry):
        one, two, total = jnp.int32(0), jnp.int32(0), jnp.int32(0)
        for p in range(NBLK * BEAM):
            two = jnp.where(sl[p % BEAM, p // BEAM] == c, p, two)
            total = total + jnp.where(sl[p % BEAM, p // BEAM] == c, 1, 0)
        for p in reversed(range(NBLK * BEAM)):
            one = jnp.where(sl[p % BEAM, p // BEAM] == c, p, one)
        tab[0, c] = one + 32 * two + 1024 * total
        return carry


    for load in loads[:6]:
        load.wait()
    pl.semaphore_wait(barrier, len(greeted))
    top, bottom = pl.ds(0, HALF0), pl.ds(HALF0, HALF1)
    first = take(3)
    base = take(16)
    near = take(16)

    def slot(a, b):
        return wl.at[lid(a, b, core)]

    columns = [pa, am, ap, a2]
    own = wl.at[me]
    early = [remote(own, own, first, to_ap), remote(own, own, first + 1, to_am)]
    for copy in early:
        copy.start()
    send(own, own, first + 2, to_a2)
    send(own, own, near, sib)
    for copy in early:
        copy.wait_send()
    send(own, own, base, to_bp)
    send(own, own, base + 1, to_bm)
    loads[6].wait()
    loads[7].wait()
    loads[8].wait()
    hidden_chunk(0)

    def spread(j):
        held = slot(columns[j], pb)
        send(held, held, base + 4 * j, to_bp)
        send(held, held, base + 4 * j + 1, to_bm)
        send(held, held, near + j, sib)

    def forward(j):
        a = columns[j]
        held = slot(a, bm)
        landed(held, base + 4 * j)
        send(held.at[top], held.at[top], base + 4 * j + 2, to_bp)
        send(held, held, near + 4 + j, sib)
        held = slot(a, bp)
        landed(held, base + 4 * j + 1)
        send(held.at[bottom], held.at[bottom], base + 4 * j + 3, to_bm)
        send(held, held, near + 8 + j, sib)

    landed(slot(am, pb), first)
    spread(1)
    landed(slot(ap, pb), first + 1)
    spread(2)
    forward(0)
    landed(slot(a2, pb), first + 2)
    spread(3)
    share_chunk(0)
    hidden_chunk(1)
    forward(1)
    share_chunk(1)
    hidden_chunk(2)
    forward(2)
    share_chunk(2)
    hidden_chunk(3)
    forward(3)
    share_chunk(3)
    for j in (0, 1, 2, 3):
        held = slot(columns[j], b2)
        landed(held.at[top], base + 4 * j + 2)
        landed(held.at[bottom], base + 4 * j + 3)
        send(held, held, near + 12 + j, sib)
        if j == 1:
            lax.fori_loop(0, 32, name_pairs, 0)
            for c in range(32, LB):
                tab[0, c] = 0
    for i in range(16):
        landed(own, near + i)

    tabled = take()
    send(tab, tab_s, tabled, sib)

    place = lax.broadcasted_iota(jnp.int32, (SB, LB), 1)

    lent = take(16)

    def lend_gl(b):
        rows = pl.ds(pl.multiple_of(b * BEAM, BEAM), BEAM)
        return remote(gl.at[rows], gl_s.at[rows], lent + b, sib)

    def lend_gh(b):
        rows = pl.ds(pl.multiple_of(b * SB, SB), SB)
        return remote(gh.at[rows], gh_s.at[rows], lent + 8 + b, sib)

    def block(b, carry):
        wanted = pos[b]
        for k in range(BEAM):
            c = sl[k, b]
            for j in range(D // LB):
                w4[k * LB:(k + 1) * LB, j * LB:(j + 1) * LB] = wl[c, j * LB:(j + 1) * LB, :]
        scores = lax.dot_general(
            hid[b], w4[...], (((1,), (1,)), ((), ())), preferred_element_type=F32
        )
        parts = []
        for k in range(BEAM):
            c = sl[k, b]
            ends = wl[c, D:SHARD, :].astype(F32)
            scale = ends[0:1] / ends[1:2]
            logits = scores[:, k * LB:(k + 1) * LB]
            hit = wanted[:, 0:1] == place + k * LB
            for column in range(1, wanted.shape[1]):
                hit = hit | (wanted[:, column:column + 1] == place + k * LB)
            target = jnp.where(hit, 1.0, 0.0)
            part = (scale * (jax.nn.sigmoid(logits) - target) / SB).astype(BF16)
            gl[b * BEAM + k] = part
            parts.append(part)

        @pl.when(b > 0)
        def _():
            lend_gl(b - 1).start()
            lend_gh(b - 1).start()

        total = jnp.dot(jnp.concatenate(parts, axis=1), w4[...], preferred_element_type=F32)
        gh[pl.ds(pl.multiple_of(b * SB, SB), SB), :] = total.astype(BF16)
        return carry

    lax.fori_loop(0, NBLK, block, 0)

    lend_gl(NBLK - 1).start()

    mid = D // 2

    def proj_part(left, right, j, n):
        rows = pl.ds(pl.multiple_of(core * mid, 16), mid)
        whole = jnp.concatenate([left[i, rows, :] for i in range(4)], axis=1)
        return jnp.dot(whole, right[:, j * LB:(j + n) * LB], preferred_element_type=F32)

    value = proj_part(enct, gh, 0, 2)
    lend_gh(NBLK - 1).start()
    for j in range(2):
        pf[j * mid:(j + 1) * mid, :] = value[:, j * LB:(j + 1) * LB]
    value = proj_part(enct, gh, 2, 4)
    for j in range(4):
        pf[(j + 2) * mid:(j + 3) * mid, :] = value[:, j * LB:(j + 1) * LB]
    for i in range(4):
        landed(enct_s.at[i], share + 2 * i + 1)

    def arrive_gh(b, carry):
        lend_gh(b).wait_recv()
        return carry

    lax.fori_loop(0, NBLK, arrive_gh, 0)
    value = proj_part(enct_s, gh_s, 0, 6)
    for j in range(6):
        rows = slice(j * mid, (j + 1) * mid)
        pf[rows, :] = pf[rows, :] + value[:, j * LB:(j + 1) * LB]

    def ablk(a):
        return pl.ds(pl.multiple_of(a * ABLK, 16), ABLK)

    pm = take(3)
    mine = ablk(pa)
    pas[2] = pf[ablk(a2), :].astype(BF16)
    pas[0] = pf[ablk(ap), :].astype(BF16)
    pas[1] = pf[ablk(am), :].astype(BF16)
    for i in range(4):
        landed(hidt_s.at[pl.ds(2 * i, 2)], share + 2 * i)
    landed(tab_s, tabled)

    def arrive_gl(b, carry):
        lend_gl(b).wait_recv()
        return carry

    lax.fori_loop(0, NBLK, arrive_gl, 0)
    send(pas.at[2], pra.at[2], pm + 2, to_a2)
    send(pas.at[0], pra.at[0], pm, to_ap)
    send(pas.at[1], pra.at[1], pm + 1, to_am)

    hm = take(12)

    def along_a(db, r):
        return remote(cb.at[db * 3 + r], ra.at[r, db], hm + db * 3 + r, (to_ap, to_am, to_a2)[r])

    def halves(c, table, turned, grads):
        code = table[0, c]
        one = lax.rem(code, 32)
        two = lax.rem(lax.div(code, 32), 32)
        total = lax.div(code, 1024)
        up = grads[one].astype(F32) * jnp.minimum(total, 1).astype(F32)
        down = grads[two].astype(F32) * jnp.maximum(total - 1, 0).astype(F32)
        left = [turned[lax.div(one, BEAM)], turned[lax.div(two, BEAM)]]
        return left, [up.astype(BF16), down.astype(BF16)]

    def own_clusters(db, carry):
        def value_of(da):
            c = lid((pa + 6 - da) % 4, (pb + 6 - db) % 4, core)
            left, right = halves(c, tab, hidt, gl)
            left_s, right_s = halves(c, tab_s, hidt_s, gl_s)
            return jnp.dot(
                jnp.concatenate(left + left_s, axis=1),
                jnp.concatenate(right + right_s, axis=0),
                preferred_element_type=F32,
            )

        cb[db * 3 + 2] = value_of(0).astype(BF16)
        cb[db * 3] = value_of(1).astype(BF16)
        along_a(db, 2).start()
        cb[db * 3 + 1] = value_of(3).astype(BF16)
        along_a(db, 0).start()
        cf[db] = value_of(2)
        along_a(db, 1).start()
        return carry

    lax.fori_loop(0, 2, own_clusters, 0)
    lax.fori_loop(3, 4, own_clusters, 0)

    def enc_chunk(i):
        rows = pl.ds(256 * i, 256)
        ge[rows, :] = lax.dot_general(
            gh[rows, :], proj[...], (((1,), (1,)), ((), ())), preferred_element_type=F32
        )

    for r in range(3):
        landed(pra.at[r], pm + r)
    value = pf[mine, :] + pra[0].astype(F32) + pra[1].astype(F32) + pra[2].astype(F32)
    pf[mine, :] = value
    pbs[...] = value.astype(BF16)

    def piece(b):
        return pl.ds(pl.multiple_of(b * PIECE, 16), PIECE)

    pn = take(3)
    lax.fori_loop(2, 3, own_clusters, 0)
    send(pbs.at[piece(b2)], prb.at[2], pn + 2, to_b2)
    send(pbs.at[piece(bp)], prb.at[0], pn, to_bp)
    send(pbs.at[piece(bm)], prb.at[1], pn + 1, to_bm)
    hn = take(3)
    enc_chunk(0)
    enc_chunk(1)

    def finish_a(db):
        for r in range(3):
            landed(ra.at[r, db], hm + db * 3 + r)
        return cf[db] + ra[0, db].astype(F32) + ra[1, db].astype(F32) + ra[2, db].astype(F32)

    for r in range(3):
        landed(prb.at[r], pn + r)
    spot_rows = pl.ds(pl.multiple_of(pa * ABLK + pb * PIECE, 16), PIECE)
    value = pf[spot_rows, :] + prb[0].astype(F32) + prb[1].astype(F32) + prb[2].astype(F32)
    ez[...] = value.astype(BF16)
    zp[z] = value.astype(BF16)
    pz = take(NZ)
    dbs[2] = finish_a(0).astype(BF16)
    for dz in (4, 3, 5, 2, 6, 1, 7):
        send(ez, zp.at[z], pz + dz, to_z[dz])
    enc_chunk(2)
    send(dbs.at[2], rbb.at[2], hn + 2, to_b2)
    dbs[0] = finish_a(1).astype(BF16)
    enc_chunk(3)
    send(dbs.at[0], rbb.at[0], hn, to_bp)
    dbs[1] = finish_a(3).astype(BF16)
    for dz in range(1, NZ):
        landed(zp.at[(z + NZ - dz) % NZ], pz + dz)
    send(dbs.at[1], rbb.at[1], hn + 1, to_bm)
    total = zp[0].astype(F32)
    for i in range(1, NZ):
        total = total + zp[i].astype(F32)

    def spot(a, b):
        return po.at[pl.ds(pl.multiple_of((core * 4 + a) * ABLK + b * PIECE, 16), PIECE)]

    po[pl.ds(pl.multiple_of((core * 4 + pa) * ABLK + pb * PIECE, 16), PIECE), :] = total.astype(BF16)
    g1 = take(3)
    g2 = take(12)
    g3 = take(16)
    along = [pb, bm, bp, b2]
    hops = [am, ap, a2]

    def outward(q):
        held = spot(pa, along[q])
        for r, device in enumerate((to_ap, to_am, to_a2)):
            send(held, held, g2 + 3 * q + r, device)
        send(held, held, g3 + q, sib)

    held = spot(pa, pb)
    for r, device in enumerate((to_bp, to_bm, to_b2)):
        send(held, held, g1 + r, device)
    outward(0)
    value = finish_a(2)
    for r in (2, 0, 1):
        landed(rbb.at[r], hn + r)
    value = value + rbb[0].astype(F32) + rbb[1].astype(F32) + rbb[2].astype(F32)
    value = value.reshape(NZ, D // NZ, LB)
    zs[...] = value.astype(BF16)
    ef[...] = value
    hz = take(NZ)
    for dz in (4, 3, 5, 2, 6, 1, 7):
        send(zs.at[(z + dz) % NZ], zr.at[dz], hz + dz, to_z[dz])
    for q in (1, 2, 3):
        landed(spot(pa, along[q]), g1 + q - 1)
        outward(q)
    for q in range(4):
        for r in range(3):
            held = spot(hops[r], along[q])
            landed(held, g2 + 3 * q + r)
            send(held, held, g3 + 4 + 3 * q + r, sib)
    for dz in range(1, NZ):
        landed(zr.at[dz], hz + dz)
    value = ef[z]
    for dz in range(1, NZ):
        value = value + zr[dz].astype(F32)
    gh_out[...] = value

    def widen(which):
        for j in range(6):
            rows = pl.ds(pl.multiple_of(which * CORE + j * mid, 16), mid)
            spread_rows = pl.ds(pl.multiple_of(which * mid, 16), mid)
            gp_out[spread_rows, j * LB:(j + 1) * LB] = po[rows, :].astype(F32)

    widen(core)
    for i in range(16):
        landed(spot(pa, pb), g3 + i)
    widen(other)
    for copy in sent:
        copy.wait_send()

    def drain(i, carry):
        lend_gl(i).wait_send()
        lend_gh(i).wait_send()
        return carry

    lax.fori_loop(0, NBLK, drain, 0)

    def drain_a(db, carry):
        for r in range(3):
            along_a(db, r).wait_send()
        return carry

    lax.fori_loop(0, 4, drain_a, 0)
    assert count[0] <= MESSAGES, count[0]


MESSAGES = 160


def scratch():
    v = pltpu.VMEM
    return [
        v((1, LB), jnp.int32), v((1, LB), jnp.int32), v((8, ROWS), jnp.int32),
        v((ROWS, D), BF16), v((D, D), BF16),
        v((32, SHARD, LB), BF16), v((NBLK, SB, 8), jnp.int32),
        v((NBLK, SB, D), BF16), v((NBLK, D, SB), BF16), v((NBLK, D, SB), BF16),
        v((4, D, ROWS // 4), BF16), v((4, D, ROWS // 4), BF16),
        v((BEAM * LB, D), BF16), v((32, SB, LB), BF16), v((32, SB, LB), BF16),
        v((ROWS, D), BF16), v((ROWS, D), BF16),
        v((12, D, LB), BF16), v((4, D, LB), F32),
        v((3, 4, D, LB), BF16), v((3, D, LB), BF16), v((3, D, LB), BF16),
        v((NZ, D // NZ, LB), F32), v((NZ, D // NZ, LB), BF16), v((NZ, D // NZ, LB), BF16),
        v((CORE, LB), F32),
        v((3, ABLK, LB), BF16), v((3, ABLK, LB), BF16),
        v((ABLK, LB), BF16), v((3, PIECE, LB), BF16),
        v((PIECE, LB), BF16), v((NZ, PIECE, LB), BF16), v((2 * CORE, LB), BF16),
        pltpu.SMEM((1, 128), jnp.int32), pltpu.SMEM((1, 128), jnp.int32),
        pltpu.SemaphoreType.DMA((MESSAGES,)), pltpu.SemaphoreType.DMA((MESSAGES,)),
        pltpu.SemaphoreType.DMA((12,)),
    ]


def shards(enc, proj, head_weight, shortlist, positives, weight_num, weight_den):
    smem = pl.BlockSpec(memory_space=pltpu.SMEM)
    vmem = pl.BlockSpec(memory_space=pltpu.VMEM)
    grad_enc, grad_proj, grad_head = pl.pallas_call(
        kernel,
        out_shape=(
            pltpu.VMEM((ROWS, D), F32),
            pltpu.VMEM((D, D), F32),
            pltpu.VMEM((D // NZ, LB), F32),
        ),
        in_specs=[smem] + [pl.BlockSpec(memory_space=pltpu.HBM)] * 6,
        out_specs=(vmem, vmem, vmem),
        scratch_shapes=scratch(),
        compiler_params=pltpu.CompilerParams(
            collective_id=0, has_side_effects=True, vmem_limit_bytes=56 << 20
        ),
    )(
        shortlist.T, weight_num.reshape(1, LB), weight_den.reshape(1, LB), positives.T,
        enc, proj, head_weight,
    )
    return (grad_enc, grad_proj, grad_head.T)


def solution(mesh):
    placed = (
        P(("dp", "label"), None),
        P(),
        P("label", None),
        P(("dp", "label"), None),
        P(("dp", "label"), None),
        P("label"),
        P("label"),
    )
    return jax.shard_map(
        shards,
        mesh=mesh,
        in_specs=placed,
        out_specs=(P(("dp", "label"), None), P(), P("label", "dp")),
        check_vma=False,
    )
```

```python
import jax
import jax.numpy as jnp
from jax import lax
from jax.experimental import pallas as pl
from jax.experimental.pallas import tpu as pltpu
from jax.sharding import PartitionSpec as P

MESH = pl.DeviceIdType.MESH
F32 = jnp.float32
BF16 = jnp.bfloat16

D = 768
LB = 128
SB = 128
BEAM = 4
NBLK = 8
ROWS = NBLK * SB
SHARD = D + 16
HALF0, HALF1 = 400, 384
NZ = 8
PIECE = 144
ABLK = 4 * PIECE
CORE = 4 * ABLK


def lid(pa, pb, core):
    xx = pa + core * (pb - pa)
    yy = pb + core * (pa - pb)
    return (yy * 4 + xx) * 2 + core


def kernel(
    sl, num_in, den_in, post_in, enc_in, proj_in, head_in,
    ge, gp_out, gh_out,
    num, den, post, enc, proj, wl, pos, hid, hidt, hidt_s, enct, enct_s, w4, gl, gl_s, gh, gh_s,
    cb, cf, ra, dbs, rbb, ef, zs, zr,
    pf, pas, pra, pbs, prb, ez, zp, po, tab, tab_s,
    ss, rs, ls,
):
    z = lax.axis_index("dp")
    me = lax.axis_index("label")
    core = me % 2
    x = (me // 2) % 4
    y = me // 8
    pa = x + core * (y - x)
    pb = y + core * (x - y)
    other = 1 - core
    ap, am, a2 = (pa + 1) % 4, (pa + 3) % 4, (pa + 2) % 4
    bp, bm, b2 = (pb + 1) % 4, (pb + 3) % 4, (pb + 2) % 4
    sib = {"label": me + 1 - 2 * core}
    to_ap = {"label": lid(ap, pb, core)}
    to_am = {"label": lid(am, pb, core)}
    to_a2 = {"label": lid(a2, pb, core)}
    to_bp = {"label": lid(pa, bp, core)}
    to_bm = {"label": lid(pa, bm, core)}
    to_b2 = {"label": lid(pa, b2, core)}
    to_z = [None] + [{"dp": (z + dz) % NZ} for dz in range(1, NZ)]

    barrier = pltpu.get_barrier_semaphore()
    greeted = [sib, to_ap, to_am, to_a2, to_bp, to_bm, to_b2] + to_z[1:]
    for device in greeted:
        pl.semaphore_signal(barrier, inc=1, device_id=device, device_id_type=MESH)

    loads = []
    for j in range(D // LB):
        loads.append(pltpu.make_async_copy(
            head_in.at[:, pl.ds(j * LB, LB)], wl.at[me, pl.ds(j * LB, LB)], ls.at[j]))
    loads.append(pltpu.make_async_copy(proj_in, proj, ls.at[6]))
    loads.append(pltpu.make_async_copy(enc_in, enc, ls.at[7]))
    small = [
        pltpu.make_async_copy(num_in, num, ls.at[8]),
        pltpu.make_async_copy(den_in, den, ls.at[9]),
    ]
    loads.append(pltpu.make_async_copy(post_in, post, ls.at[10]))
    for load in small + loads:
        load.start()
    for load in small:
        load.wait()
    line = lax.broadcasted_iota(jnp.int32, (16, LB), 0)
    tail = jnp.where(line == 0, num[...], jnp.where(line == 1, den[...], 1))
    wl[me, D:SHARD, :] = tail.astype(F32).astype(BF16)

    count = [0]
    sent = []

    def take(n=1):
        first = count[0]
        count[0] += n
        return first

    def remote(src, dst, i, device):
        return pltpu.make_async_remote_copy(
            src_ref=src, dst_ref=dst, send_sem=ss.at[i], recv_sem=rs.at[i],
            device_id=device, device_id_type=MESH,
        )

    def send(src, dst, i, device):
        copy = remote(src, dst, i, device)
        copy.start()
        sent.append(copy)

    def landed(dst, i):
        remote(dst, dst, i, sib).wait_recv()

    def hidden_chunk(i):
        for b in (2 * i, 2 * i + 1):
            pos[b] = post[:, b * SB:(b + 1) * SB].T
        rows = enc[pl.ds(256 * i, 256), :]
        value = jnp.dot(rows, proj[...], preferred_element_type=F32).astype(BF16)
        hid[2 * i] = value[:SB]
        hid[2 * i + 1] = value[SB:]
        hidt[2 * i] = value[:SB].T
        hidt[2 * i + 1] = value[SB:].T
        enct[i] = rows.T

    share = take(8)

    def share_chunk(i):
        pair = pl.ds(2 * i, 2)
        send(hidt.at[pair], hidt_s.at[pair], share + 2 * i, sib)
        send(enct.at[i], enct_s.at[i], share + 2 * i + 1, sib)

    def name_pairs(c, carry):
        one, two, total = jnp.int32(0), jnp.int32(0), jnp.int32(0)
        for p in range(NBLK * BEAM):
            two = jnp.where(sl[p % BEAM, p // BEAM] == c, p, two)
            total = total + jnp.where(sl[p % BEAM, p // BEAM] == c, 1, 0)
        for p in reversed(range(NBLK * BEAM)):
            one = jnp.where(sl[p % BEAM, p // BEAM] == c, p, one)
        tab[0, c] = one + 32 * two + 1024 * total
        return carry


    for load in loads[:6]:
        load.wait()
    pl.semaphore_wait(barrier, len(greeted))
    top, bottom = pl.ds(0, HALF0), pl.ds(HALF0, HALF1)
    first = take(3)
    base = take(16)
    near = take(16)

    def slot(a, b):
        return wl.at[lid(a, b, core)]

    columns = [pa, am, ap, a2]
    own = wl.at[me]
    early = [remote(own, own, first, to_ap), remote(own, own, first + 1, to_am)]
    for copy in early:
        copy.start()
    send(own, own, first + 2, to_a2)
    send(own, own, near, sib)
    for copy in early:
        copy.wait_send()
    send(own, own, base, to_bp)
    send(own, own, base + 1, to_bm)
    loads[6].wait()
    loads[7].wait()
    loads[8].wait()
    hidden_chunk(0)

    def spread(j):
        held = slot(columns[j], pb)
        send(held, held, base + 4 * j, to_bp)
        send(held, held, base + 4 * j + 1, to_bm)
        send(held, held, near + j, sib)

    def forward(j):
        a = columns[j]
        held = slot(a, bm)
        landed(held, base + 4 * j)
        send(held.at[top], held.at[top], base + 4 * j + 2, to_bp)
        send(held, held, near + 4 + j, sib)
        held = slot(a, bp)
        landed(held, base + 4 * j + 1)
        send(held.at[bottom], held.at[bottom], base + 4 * j + 3, to_bm)
        send(held, held, near + 8 + j, sib)

    landed(slot(am, pb), first)
    spread(1)
    landed(slot(ap, pb), first + 1)
    spread(2)
    forward(0)
    landed(slot(a2, pb), first + 2)
    spread(3)
    share_chunk(0)
    hidden_chunk(1)
    forward(1)
    share_chunk(1)
    hidden_chunk(2)
    forward(2)
    share_chunk(2)
    hidden_chunk(3)
    forward(3)
    share_chunk(3)
    for j in (0, 1, 2, 3):
        held = slot(columns[j], b2)
        landed(held.at[top], base + 4 * j + 2)
        landed(held.at[bottom], base + 4 * j + 3)
        send(held, held, near + 12 + j, sib)
        if j == 1:
            lax.fori_loop(0, 32, name_pairs, 0)
            for c in range(32, LB):
                tab[0, c] = 0
    for i in range(16):
        landed(own, near + i)

    tabled = take()
    send(tab, tab_s, tabled, sib)

    place = lax.broadcasted_iota(jnp.int32, (SB, LB), 1)

    lent = take(16)

    def lend_gl(b):
        rows = pl.ds(pl.multiple_of(b * BEAM, BEAM), BEAM)
        return remote(gl.at[rows], gl_s.at[rows], lent + b, sib)

    def lend_gh(b):
        rows = pl.ds(pl.multiple_of(b * SB, SB), SB)
        return remote(gh.at[rows], gh_s.at[rows], lent + 8 + b, sib)

    def block(b, carry):
        wanted = pos[b]
        for k in range(BEAM):
            c = sl[k, b]
            for j in range(D // LB):
                w4[k * LB:(k + 1) * LB, j * LB:(j + 1) * LB] = wl[c, j * LB:(j + 1) * LB, :]
        scores = lax.dot_general(
            hid[b], w4[...], (((1,), (1,)), ((), ())), preferred_element_type=F32
        )
        parts = []
        for k in range(BEAM):
            c = sl[k, b]
            ends = wl[c, D:SHARD, :].astype(F32)
            scale = ends[0:1] / ends[1:2]
            logits = scores[:, k * LB:(k + 1) * LB]
            hit = wanted[:, 0:1] == place + k * LB
            for column in range(1, wanted.shape[1]):
                hit = hit | (wanted[:, column:column + 1] == place + k * LB)
            target = jnp.where(hit, 1.0, 0.0)
            part = (scale * (jax.nn.sigmoid(logits) - target) / SB).astype(BF16)
            gl[b * BEAM + k] = part
            parts.append(part)

        @pl.when(b > 0)
        def _():
            lend_gl(b - 1).start()
            lend_gh(b - 1).start()

        total = jnp.dot(jnp.concatenate(parts, axis=1), w4[...], preferred_element_type=F32)
        gh[pl.ds(pl.multiple_of(b * SB, SB), SB), :] = total.astype(BF16)
        return carry

    lax.fori_loop(0, NBLK, block, 0)

    lend_gl(NBLK - 1).start()

    mid = D // 2

    def proj_part(left, right, j, n):
        rows = pl.ds(pl.multiple_of(core * mid, 16), mid)
        whole = jnp.concatenate([left[i, rows, :] for i in range(4)], axis=1)
        return jnp.dot(whole, right[:, j * LB:(j + n) * LB], preferred_element_type=F32)

    value = proj_part(enct, gh, 0, 2)
    lend_gh(NBLK - 1).start()
    for j in range(2):
        pf[j * mid:(j + 1) * mid, :] = value[:, j * LB:(j + 1) * LB]
    value = proj_part(enct, gh, 2, 4)
    for j in range(4):
        pf[(j + 2) * mid:(j + 3) * mid, :] = value[:, j * LB:(j + 1) * LB]
    for i in range(4):
        landed(enct_s.at[i], share + 2 * i + 1)

    def arrive_gh(b, carry):
        lend_gh(b).wait_recv()
        return carry

    lax.fori_loop(0, NBLK, arrive_gh, 0)
    value = proj_part(enct_s, gh_s, 0, 6)
    for j in range(6):
        rows = slice(j * mid, (j + 1) * mid)
        pf[rows, :] = pf[rows, :] + value[:, j * LB:(j + 1) * LB]

    def ablk(a):
        return pl.ds(pl.multiple_of(a * ABLK, 16), ABLK)

    pm = take(3)
    mine = ablk(pa)
    pas[2] = pf[ablk(a2), :].astype(BF16)
    pas[0] = pf[ablk(ap), :].astype(BF16)
    pas[1] = pf[ablk(am), :].astype(BF16)
    for i in range(4):
        landed(hidt_s.at[pl.ds(2 * i, 2)], share + 2 * i)
    landed(tab_s, tabled)

    def arrive_gl(b, carry):
        lend_gl(b).wait_recv()
        return carry

    lax.fori_loop(0, NBLK, arrive_gl, 0)
    send(pas.at[2], pra.at[2], pm + 2, to_a2)
    send(pas.at[0], pra.at[0], pm, to_ap)
    send(pas.at[1], pra.at[1], pm + 1, to_am)

    hm = take(12)

    def along_a(db, r):
        return remote(cb.at[db * 3 + r], ra.at[r, db], hm + db * 3 + r, (to_ap, to_am, to_a2)[r])

    def halves(c, table, turned, grads):
        code = table[0, c]
        one = lax.rem(code, 32)
        two = lax.rem(lax.div(code, 32), 32)
        total = lax.div(code, 1024)
        up = grads[one].astype(F32) * jnp.minimum(total, 1).astype(F32)
        down = grads[two].astype(F32) * jnp.maximum(total - 1, 0).astype(F32)
        left = [turned[lax.div(one, BEAM)], turned[lax.div(two, BEAM)]]
        return left, [up.astype(BF16), down.astype(BF16)]

    def own_clusters(db, carry):
        def value_of(da):
            c = lid((pa + 6 - da) % 4, (pb + 6 - db) % 4, core)
            left, right = halves(c, tab, hidt, gl)
            left_s, right_s = halves(c, tab_s, hidt_s, gl_s)
            return jnp.dot(
                jnp.concatenate(left + left_s, axis=1),
                jnp.concatenate(right + right_s, axis=0),
                preferred_element_type=F32,
            )

        cb[db * 3 + 2] = value_of(0).astype(BF16)
        cb[db * 3] = value_of(1).astype(BF16)
        along_a(db, 2).start()
        cb[db * 3 + 1] = value_of(3).astype(BF16)
        along_a(db, 0).start()
        cf[db] = value_of(2)
        along_a(db, 1).start()
        return carry

    lax.fori_loop(0, 2, own_clusters, 0)
    lax.fori_loop(3, 4, own_clusters, 0)
    lax.fori_loop(2, 3, own_clusters, 0)

    def enc_chunk(i):
        rows = pl.ds(256 * i, 256)
        ge[rows, :] = lax.dot_general(
            gh[rows, :], proj[...], (((1,), (1,)), ((), ())), preferred_element_type=F32
        )

    for r in range(3):
        landed(pra.at[r], pm + r)
    value = pf[mine, :] + pra[0].astype(F32) + pra[1].astype(F32) + pra[2].astype(F32)
    pbs[...] = value.astype(BF16)
    pf[mine, :] = value

    def piece(b):
        return pl.ds(pl.multiple_of(b * PIECE, 16), PIECE)

    pn = take(3)
    send(pbs.at[piece(b2)], prb.at[2], pn + 2, to_b2)
    send(pbs.at[piece(bp)], prb.at[0], pn, to_bp)
    send(pbs.at[piece(bm)], prb.at[1], pn + 1, to_bm)
    hn = take(3)
    enc_chunk(0)
    enc_chunk(1)

    def finish_a(db):
        for r in range(3):
            landed(ra.at[r, db], hm + db * 3 + r)
        return cf[db] + ra[0, db].astype(F32) + ra[1, db].astype(F32) + ra[2, db].astype(F32)

    for r in range(3):
        landed(prb.at[r], pn + r)
    spot_rows = pl.ds(pl.multiple_of(pa * ABLK + pb * PIECE, 16), PIECE)
    value = pf[spot_rows, :] + prb[0].astype(F32) + prb[1].astype(F32) + prb[2].astype(F32)
    ez[...] = value.astype(BF16)
    zp[z] = value.astype(BF16)
    pz = take(NZ)
    dbs[2] = finish_a(0).astype(BF16)
    for dz in (4, 3, 5, 2, 6, 1, 7):
        send(ez, zp.at[z], pz + dz, to_z[dz])
    enc_chunk(2)
    send(dbs.at[2], rbb.at[2], hn + 2, to_b2)
    dbs[0] = finish_a(1).astype(BF16)
    enc_chunk(3)
    send(dbs.at[0], rbb.at[0], hn, to_bp)
    dbs[1] = finish_a(3).astype(BF16)
    for dz in range(1, NZ):
        landed(zp.at[(z + NZ - dz) % NZ], pz + dz)
    send(dbs.at[1], rbb.at[1], hn + 1, to_bm)
    total = zp[0].astype(F32)
    for i in range(1, NZ):
        total = total + zp[i].astype(F32)

    def spot(a, b):
        return po.at[pl.ds(pl.multiple_of((core * 4 + a) * ABLK + b * PIECE, 16), PIECE)]

    po[pl.ds(pl.multiple_of((core * 4 + pa) * ABLK + pb * PIECE, 16), PIECE), :] = total.astype(BF16)
    g1 = take(3)
    g2 = take(12)
    g3 = take(16)
    along = [pb, bm, bp, b2]
    hops = [am, ap, a2]

    def outward(q):
        held = spot(pa, along[q])
        for r, device in enumerate((to_ap, to_am, to_a2)):
            send(held, held, g2 + 3 * q + r, device)
        send(held, held, g3 + q, sib)

    held = spot(pa, pb)
    for r, device in enumerate((to_bp, to_bm, to_b2)):
        send(held, held, g1 + r, device)
    outward(0)
    value = finish_a(2)
    for r in (2, 0, 1):
        landed(rbb.at[r], hn + r)
    value = value + rbb[0].astype(F32) + rbb[1].astype(F32) + rbb[2].astype(F32)
    value = value.reshape(NZ, D // NZ, LB)
    zs[...] = value.astype(BF16)
    ef[...] = value
    hz = take(NZ)
    for dz in (4, 3, 5, 2, 6, 1, 7):
        send(zs.at[(z + dz) % NZ], zr.at[dz], hz + dz, to_z[dz])
    for q in (1, 2, 3):
        landed(spot(pa, along[q]), g1 + q - 1)
        outward(q)
    for q in range(4):
        for r in range(3):
            held = spot(hops[r], along[q])
            landed(held, g2 + 3 * q + r)
            send(held, held, g3 + 4 + 3 * q + r, sib)
    for dz in range(1, NZ):
        landed(zr.at[dz], hz + dz)
    value = ef[z]
    for dz in range(1, NZ):
        value = value + zr[dz].astype(F32)
    gh_out[...] = value

    def widen(which):
        for j in range(6):
            rows = pl.ds(pl.multiple_of(which * CORE + j * mid, 16), mid)
            spread_rows = pl.ds(pl.multiple_of(which * mid, 16), mid)
            gp_out[spread_rows, j * LB:(j + 1) * LB] = po[rows, :].astype(F32)

    widen(core)
    for i in range(16):
        landed(spot(pa, pb), g3 + i)
    widen(other)
    for copy in sent:
        copy.wait_send()

    def drain(i, carry):
        lend_gl(i).wait_send()
        lend_gh(i).wait_send()
        return carry

    lax.fori_loop(0, NBLK, drain, 0)

    def drain_a(db, carry):
        for r in range(3):
            along_a(db, r).wait_send()
        return carry

    lax.fori_loop(0, 4, drain_a, 0)
    assert count[0] <= MESSAGES, count[0]


MESSAGES = 160


def scratch():
    v = pltpu.VMEM
    return [
        v((1, LB), jnp.int32), v((1, LB), jnp.int32), v((8, ROWS), jnp.int32),
        v((ROWS, D), BF16), v((D, D), BF16),
        v((32, SHARD, LB), BF16), v((NBLK, SB, 8), jnp.int32),
        v((NBLK, SB, D), BF16), v((NBLK, D, SB), BF16), v((NBLK, D, SB), BF16),
        v((4, D, ROWS // 4), BF16), v((4, D, ROWS // 4), BF16),
        v((BEAM * LB, D), BF16), v((32, SB, LB), BF16), v((32, SB, LB), BF16),
        v((ROWS, D), BF16), v((ROWS, D), BF16),
        v((12, D, LB), BF16), v((4, D, LB), F32),
        v((3, 4, D, LB), BF16), v((3, D, LB), BF16), v((3, D, LB), BF16),
        v((NZ, D // NZ, LB), F32), v((NZ, D // NZ, LB), BF16), v((NZ, D // NZ, LB), BF16),
        v((CORE, LB), F32),
        v((3, ABLK, LB), BF16), v((3, ABLK, LB), BF16),
        v((ABLK, LB), BF16), v((3, PIECE, LB), BF16),
        v((PIECE, LB), BF16), v((NZ, PIECE, LB), BF16), v((2 * CORE, LB), BF16),
        pltpu.SMEM((1, 128), jnp.int32), pltpu.SMEM((1, 128), jnp.int32),
        pltpu.SemaphoreType.DMA((MESSAGES,)), pltpu.SemaphoreType.DMA((MESSAGES,)),
        pltpu.SemaphoreType.DMA((12,)),
    ]


def shards(enc, proj, head_weight, shortlist, positives, weight_num, weight_den):
    smem = pl.BlockSpec(memory_space=pltpu.SMEM)
    vmem = pl.BlockSpec(memory_space=pltpu.VMEM)
    grad_enc, grad_proj, grad_head = pl.pallas_call(
        kernel,
        out_shape=(
            pltpu.VMEM((ROWS, D), F32),
            pltpu.VMEM((D, D), F32),
            pltpu.VMEM((D // NZ, LB), F32),
        ),
        in_specs=[smem] + [pl.BlockSpec(memory_space=pltpu.HBM)] * 6,
        out_specs=(vmem, vmem, vmem),
        scratch_shapes=scratch(),
        compiler_params=pltpu.CompilerParams(
            collective_id=0, has_side_effects=True, vmem_limit_bytes=56 << 20
        ),
    )(
        shortlist.T, weight_num.reshape(1, LB), weight_den.reshape(1, LB), positives.T,
        enc, proj, head_weight,
    )
    return (grad_enc, grad_proj, grad_head.T)


def solution(mesh):
    placed = (
        P(("dp", "label"), None),
        P(),
        P("label", None),
        P(("dp", "label"), None),
        P(("dp", "label"), None),
        P("label"),
        P("label"),
    )
    return jax.shard_map(
        shards,
        mesh=mesh,
        in_specs=placed,
        out_specs=(P(("dp", "label"), None), P(), P("label", "dp")),
        check_vma=False,
    )
```
